512 devices in a mesh: section: 16 (over y, x_hi, core), expert: 32 (over x_lo, z).
Axes of the slice: x: 4 (x_hi: 2, x_lo: 2; x = x_hi * 2 + x_lo), y: 4, z: 16, core: 2. Of those that a mesh axis runs over, the one named last changes fastest.
Arguments:
- act_in: bfloat16 [16, 4096, 2048], P('section', 'expert'), may hold values from -6 to 6
- saved_in: bfloat16 [16, 4096, 2048], P('section', 'expert'), may hold values from -6 to 6
- grad_in: bfloat16 [16, 4096, 2048], P('section', 'expert'), may hold values from -6 to 6
- norm_gain: float32 [16, 2048], P('section'), may hold values from 0.1 to 1.9
- w_gate: bfloat16 [16, 2048, 6144], P('section', None, 'expert'), may hold values from -0.125 to 0.125
- w_up: bfloat16 [16, 2048, 6144], P('section', None, 'expert'), may hold values from -0.125 to 0.125
- w_down: bfloat16 [16, 6144, 2048], P('section', 'expert'), may hold values from -0.21875 to 0.21875
- routes_fwd: int32 [16, 4096, 1], P('section', 'expert'), may hold values from 0 to 7; in each aligned block of 128 rows (0 to 127, 128 to 255, ..., all dimensions but the last counted through in order) at most 18 rows name the same one
- gates_fwd: float32 [16, 4096, 1], P('section', 'expert'), may hold values from 0.1 to 1
- routes_bwd: int32 [16, 4096, 1], P('section', 'expert'), may hold values from 0 to 7; in each aligned block of 128 rows (0 to 127, 128 to 255, ..., all dimensions but the last counted through in order) at most 18 rows name the same one
- gates_bwd: float32 [16, 4096, 1], P('section', 'expert'), may hold values from 0.1 to 1
Outputs:
- act_out: bfloat16 [16, 4096, 2048], P('section', 'expert')
- grad_out: bfloat16 [16, 4096, 2048], P('section', 'expert')
The draws below stay inside these ranges and needn't reach their ends.
Inputs may be any that keep to these rules, and one draw needn't show every extreme that they name: `routes_fwd`: the 1 expert of a token differ; within the 128 tokens of one device no expert is named by more than 18 routes, and in some such blocks one expert is named by exactly 18. `routes_bwd`: as for routes_fwd.
All inputs are finite; a program needn't handle non-finite values.
Results may differ from the reference program's by a relative error of at most 0.005.
Values may be sent and summed in bfloat16 or wider, within the bound.
A program may use at most 64 MiB of HBM per device.

```python
import math
import jax
import jax.numpy as jnp
import numpy as np
from jax import lax

D = 2048
FF = 768
SPLIT = 4
TOPK = 1
TOK = 128
FF_DEV = 192
EXPERTS = 8
CAP = 18
TOKENS = 4096
N_SECTION = 16


def block_scale(rng, extent, split, least, high):
    def one(position, blocks):
        steps = jax.random.uniform(jax.random.fold_in(jax.random.fold_in(rng, 6), position), (blocks,), jnp.float32, least / len(split), high / len(split))
        return jnp.repeat(jnp.exp(steps), extent[position] // blocks).reshape((-1,) + (1,) * (len(extent) - position - 1))

    loudness = one(*split[0])
    for cut in split[1:]:
        loudness = loudness * one(*cut)
    return loudness


def shared_out(stream_key, own, number, rows, count, top, limit, skew):
    order = jax.random.permutation(stream_key, count)
    packed, usual = portions_of(count, rows * top, limit, skew, True), portions_of(count, rows * top, limit, skew, False)
    places = jnp.arange(count)

    def named(sizes, turn):
        used = int((sizes > 0).sum())
        fixed = max(1, used // 4)
        moved = fixed + (places - fixed + turn * (used - fixed)) % max(1, count - fixed)
        return jnp.zeros((count,), jnp.int32).at[order[jnp.where(places < fixed, places, moved)]].set(jnp.asarray(sizes, jnp.int32))

    sizes = jnp.where(number % 4 == 0, named(packed, number // 4), named(usual, number - number // 4 - 1))
    mixed = jax.random.permutation(jax.random.fold_in(own, 3), count)
    donor, sink = mixed[0:count // 2 * 2:2], mixed[1:count // 2 * 2:2]
    room = jnp.minimum(sizes[donor] - 1, limit - sizes[sink]) // 2
    room = jnp.where((donor == order[0]) | (sink == order[0]) | (sizes[sink] == 0), 0, jnp.maximum(room, 0))
    moved = jax.random.randint(jax.random.fold_in(own, 4), (count // 2,), 0, 1 << 20) % (room + 1)
    sizes = sizes.at[donor].add(-moved).at[sink].add(moved)
    items = jnp.searchsorted(jnp.cumsum(sizes), jnp.arange(rows * top), side="right").astype(jnp.int32)
    grid = items.reshape(top, rows).T
    grid = grid[jax.random.permutation(jax.random.fold_in(own, 1), rows)]
    turn = jax.random.randint(jax.random.fold_in(own, 2), (rows, 1), 0, top)
    return jnp.take_along_axis(grid, (jnp.arange(top)[None, :] + turn) % top, axis=1)


def portions_of(number_of, total, most, skew, full):
    portions = [(1 << 20) // math.isqrt(rank ** skew) + 1 for rank in range(1, number_of + 1)]
    largest = most if full else min(most, max(-(-total // number_of), total * portions[0] // sum(portions)))
    least = 1 if total - largest >= number_of - 1 else 0
    given, rest = [largest] + [least] * (number_of - 1), total - largest - least * (number_of - 1)
    while rest > 0:
        candidates = [i for i in range(1, number_of) if given[i] < largest] or [i for i in range(1, number_of) if given[i] < most]
        pool, remaining = sum([portions[i] for i in candidates]), rest
        for i in candidates:
            addition = min(most - given[i], max(1, remaining * portions[i] // pool), rest)
            given[i] = given[i] + addition
            rest = rest - addition
    return np.array(given)


def bell_draw(rng, shape, spread, bound, split=(), held_as=jnp.bfloat16):
    entries = jax.random.normal(rng, shape, jnp.float32) * spread
    if len(split) > 0:
        entries = block_scale(rng, shape, split, -0.22, 0.18) * entries
    return jnp.clip(entries, min=-bound, max=bound).astype(held_as)


def setup_inputs(seed: int = 0) -> dict:
    key_list = jax.random.split(jax.random.key(seed), 12)
    act_in = bell_draw(key_list[0], (N_SECTION, TOKENS, D), 1.0, 6.0, ((0, 16), (1, 32)))
    saved_in = bell_draw(key_list[1], (N_SECTION, TOKENS, D), 1.0, 6.0, ((0, 16), (1, 32)))
    grad_in = bell_draw(key_list[2], (N_SECTION, TOKENS, D), 1.0, 6.0, ((0, 16), (1, 32)))
    norm_gain = jnp.clip(1.0 + 0.18 * jax.random.normal(key_list[3], (N_SECTION, D), jnp.float32), 0.1, 1.9)
    w_gate = bell_draw(key_list[4], (N_SECTION, D, EXPERTS * FF), D ** -0.5, 0.125, ((0, 16), (2, 32)))
    w_up = bell_draw(key_list[5], (N_SECTION, D, EXPERTS * FF), D ** -0.5, 0.125, ((0, 16), (2, 32)))
    w_down = bell_draw(key_list[6], (N_SECTION, EXPERTS * FF, D), FF ** -0.5, 0.21875, ((0, 16), (1, 32)))
    routes_fwd_keys = jax.random.split(jax.random.fold_in(key_list[7], 1), N_SECTION * TOKENS // TOK)
    routes_fwd_turns = jax.random.permutation(jax.random.fold_in(key_list[7], 3), N_SECTION * TOKENS // TOK)
    routes_fwd = jax.vmap(lambda own, number: shared_out(jax.random.fold_in(key_list[7], 2), own, number, TOK, EXPERTS, TOPK, CAP, 2))(routes_fwd_keys, routes_fwd_turns).reshape((N_SECTION, TOKENS, TOPK))
    gates_fwd = jnp.clip(jnp.exp(math.log(1.0) - 2.3025851 * jax.random.uniform(key_list[8], (N_SECTION, TOKENS, TOPK), jnp.float32) ** block_scale(key_list[8], (N_SECTION, TOKENS, TOPK), ((0, 16), (1, 32)), -0.2, 0.2)), 0.1, 1.0)
    routes_bwd_keys = jax.random.split(jax.random.fold_in(key_list[9], 1), N_SECTION * TOKENS // TOK)
    routes_bwd_turns = jax.random.permutation(jax.random.fold_in(key_list[9], 3), N_SECTION * TOKENS // TOK)
    routes_bwd = jax.vmap(lambda own, number: shared_out(jax.random.fold_in(key_list[9], 2), own, number, TOK, EXPERTS, TOPK, CAP, 2))(routes_bwd_keys, routes_bwd_turns).reshape((N_SECTION, TOKENS, TOPK))
    gates_bwd = jnp.clip(jnp.exp(math.log(1.0) - 2.3025851 * jax.random.uniform(key_list[10], (N_SECTION, TOKENS, TOPK), jnp.float32) ** block_scale(key_list[10], (N_SECTION, TOKENS, TOPK), ((0, 16), (1, 32)), -0.2, 0.2)), 0.1, 1.0)
    return {"act_in": act_in, "saved_in": saved_in, "grad_in": grad_in, "norm_gain": norm_gain, "w_gate": w_gate, "w_up": w_up, "w_down": w_down, "routes_fwd": routes_fwd, "gates_fwd": gates_fwd, "routes_bwd": routes_bwd, "gates_bwd": gates_bwd}


norm_eps = 1e-06

def silu_parts(values):
    sigma = jax.nn.sigmoid(values)
    return (values * sigma, sigma * (1.0 + values * (1.0 - sigma)))

def normalize(block_rows, gain_row):
    values = block_rows.astype(jnp.float32)
    inv_scale = lax.rsqrt(lax.optimization_barrier(jnp.mean(values * values, axis=-1, keepdims=True)) + norm_eps)
    return (values * inv_scale * gain_row, inv_scale)

def slot_targets(routes):
    total = routes.shape[0]
    top_count = routes.shape[1]
    blocks = total // TOK
    flat_routes = routes.reshape(blocks, TOK * top_count)
    onehot = (flat_routes[:, :, None] == jnp.arange(EXPERTS, dtype=jnp.int32)[None, None, :]).astype(jnp.int32)
    before = jnp.cumsum(onehot, axis=1) - onehot
    slot_index = lax.optimization_barrier(jnp.sum(before * onehot, axis=2))
    device_index = jnp.arange(blocks, dtype=jnp.int32)[:, None]
    target = flat_routes * (blocks * CAP) + device_index * CAP + slot_index
    return target.reshape(total * top_count).astype(jnp.int32)

def section_pass(x_fwd, x_bwd, upstream, gain_row, gate_all, up_all, down_all, r_fwd, g_fwd, r_bwd, g_bwd):
    total = x_fwd.shape[0]
    slot_total = total // TOK * CAP
    n_fwd = normalize(x_fwd, gain_row)[0].astype(jnp.bfloat16)
    values_b, inv_scale = normalize(x_bwd, gain_row)
    n_bwd = values_b.astype(jnp.bfloat16)
    target_f = slot_targets(r_fwd)
    target_b = slot_targets(r_bwd)
    token_index = jnp.repeat(jnp.arange(total, dtype=jnp.int32), TOPK)
    empty = jnp.zeros((EXPERTS * slot_total, D), jnp.bfloat16)
    buffer_f = empty.at[target_f].set(n_fwd[token_index])
    buffer_b = empty.at[target_b].set(n_bwd[token_index])
    buffer_g = empty.at[target_b].set(upstream[token_index])
    outs_f = []
    outs_b = []
    for expert_id in range(EXPERTS):
        gate_w = gate_all[:, expert_id * FF:(expert_id + 1) * FF]
        up_w = up_all[:, expert_id * FF:(expert_id + 1) * FF]
        down_w = down_all[expert_id * FF:(expert_id + 1) * FF]
        lower = expert_id * slot_total
        slot_rows = buffer_f[lower:lower + slot_total]
        gate_pre = jnp.dot(slot_rows, gate_w, preferred_element_type=jnp.float32)
        up_pre = jnp.dot(slot_rows, up_w, preferred_element_type=jnp.float32)
        activation, _ = silu_parts(gate_pre)
        hidden = (activation * up_pre).astype(jnp.bfloat16)
        summed = jnp.zeros((slot_total, D), jnp.float32)
        for share in range(SPLIT):
            cut = slice(share * FF_DEV, (share + 1) * FF_DEV)
            partial_value = jnp.dot(hidden[:, cut], down_w[cut], preferred_element_type=jnp.float32).astype(jnp.bfloat16)
            summed = summed + partial_value.astype(jnp.float32)
        outs_f.append(summed)
        slot_rows = buffer_b[lower:lower + slot_total]
        grad_rows = buffer_g[lower:lower + slot_total]
        gate_pre = jnp.dot(slot_rows, gate_w, preferred_element_type=jnp.float32)
        up_pre = jnp.dot(slot_rows, up_w, preferred_element_type=jnp.float32)
        activation, derivative = silu_parts(gate_pre)
        d_hidden = jnp.dot(grad_rows, down_w.T, preferred_element_type=jnp.float32)
        d_gate = (d_hidden * up_pre * derivative).astype(jnp.bfloat16)
        d_up = (d_hidden * activation).astype(jnp.bfloat16)
        summed = jnp.zeros((slot_total, D), jnp.float32)
        for share in range(SPLIT):
            cut = slice(share * FF_DEV, (share + 1) * FF_DEV)
            partial_value = jnp.dot(d_gate[:, cut], gate_w[:, cut].T, preferred_element_type=jnp.float32)
            partial_value = partial_value + jnp.dot(d_up[:, cut], up_w[:, cut].T, preferred_element_type=jnp.float32)
            summed = summed + partial_value.astype(jnp.bfloat16).astype(jnp.float32)
        outs_b.append(summed)
    values_f = jnp.concatenate(outs_f, axis=0)
    values_bk = jnp.concatenate(outs_b, axis=0)
    mixed = lax.optimization_barrier(jnp.sum(values_f[target_f].reshape(total, TOPK, D) * g_fwd[:, :, None], axis=1))
    act_out = (x_fwd.astype(jnp.float32) + mixed).astype(jnp.bfloat16)
    d_norm = lax.optimization_barrier(jnp.sum(values_bk[target_b].reshape(total, TOPK, D) * g_bwd[:, :, None], axis=1))
    scaled = d_norm * gain_row
    base = x_bwd.astype(jnp.float32)
    d_input = inv_scale * (scaled - base * inv_scale * inv_scale * lax.optimization_barrier(jnp.mean(scaled * base, axis=-1, keepdims=True)))
    grad_out = (upstream.astype(jnp.float32) + d_input).astype(jnp.bfloat16)
    return (act_out, grad_out)

def reference(act_in, saved_in, grad_in, norm_gain, w_gate, w_up, w_down, routes_fwd, gates_fwd, routes_bwd, gates_bwd):
    sections = act_in.shape[0]
    arrived = jnp.roll(act_in, 1, axis=0)
    upstream = jnp.roll(grad_in, -1, axis=0)
    outs_a = []
    outs_g = []
    for section_id in range(sections):
        first_out, second_out = section_pass(arrived[section_id], saved_in[section_id], upstream[section_id], norm_gain[section_id], w_gate[section_id], w_up[section_id], w_down[section_id], routes_fwd[section_id], gates_fwd[section_id], routes_bwd[section_id], gates_bwd[section_id])
        outs_a.append(first_out)
        outs_g.append(second_out)
    return (jnp.stack(outs_a, axis=0), jnp.stack(outs_g, axis=0))
```

```python
import jax
import jax.numpy as jnp
from jax import lax
from jax.experimental import pallas as pl
from jax.experimental.pallas import tpu as pltpu
from jax.sharding import PartitionSpec as P

MESH = pl.DeviceIdType.MESH

SPLIT = 4
EXPERTS = 8
D = 2048
UNITS = 192
WIDE = UNITS * SPLIT
MAIN = 16
TAIL = 2
SOURCES = 16
ROWS = SOURCES * (MAIN + TAIL)
FIRST_TAIL = SOURCES * MAIN
RING = 16
BLOCKS = RING // SPLIT
TILE = 256

norm_eps = 1e-06

NT = (((1,), (1,)), ((), ()))


def passed_along(value, axis, steps):
    count = lax.axis_size(axis)
    pairs = [(source, (source + steps) % count) for source in range(count)]
    return lax.ppermute(value, axis, pairs)


def normalize(block_rows, gain_row):
    values = block_rows.astype(jnp.float32)
    inv_scale = lax.rsqrt(jnp.mean(values * values, axis=-1, keepdims=True) + norm_eps)
    return (values * inv_scale * gain_row, inv_scale)


def slot_chooser(routes):
    flat_routes = routes[:, 0]
    onehot = (flat_routes[:, None] == jnp.arange(EXPERTS, dtype=jnp.int32)[None, :]).astype(
        jnp.int32
    )
    before = jnp.cumsum(onehot, axis=0) - onehot
    slot_index = jnp.sum(before * onehot, axis=1)
    target = jnp.where(
        slot_index < MAIN,
        flat_routes * MAIN + slot_index,
        EXPERTS * MAIN + flat_routes * TAIL + slot_index - MAIN,
    )
    total = EXPERTS * (MAIN + TAIL)
    return (jnp.arange(total, dtype=jnp.int32)[:, None] == target[None, :]).astype(jnp.bfloat16)


def way(block, place, expert):
    there = expert % BLOCKS
    apart = lax.rem(there - block + BLOCKS, BLOCKS)
    low = place < 2
    member = jnp.where(
        apart == 0,
        jnp.where(low, 1, 2),
        jnp.where(apart == 1, 1, jnp.where(apart == 3, 2, jnp.where(low, 2, 1))),
    )
    odd = lax.rem(place, 2)
    kind = jnp.where(apart == 0, 6 + odd, jnp.where(apart == 2, 4 + odd, place))
    return (expert // BLOCKS) * RING + there * SPLIT + member, kind


def origin(block, place, slot):
    source_x = slot // 8
    kind = lax.rem(slot, 8)
    left = place == 1
    apart = jnp.where(kind < 4, jnp.where(left, 3, 1), jnp.where(kind < 6, 2, 0))
    source_place = jnp.where(
        kind < 4,
        kind,
        jnp.where(
            kind < 6,
            jnp.where(left, kind - 2, kind - 4),
            jnp.where(left, kind - 6, kind - 4),
        ),
    )
    source_block = lax.rem(block + apart, BLOCKS)
    return source_x * RING + source_block * SPLIT + source_place


def expert_kernel(
    f_main, f_tail, b_main, b_tail, g_main, g_tail, wg_in, wu_in, wd_in,
    of_main, of_tail, ob_main, ob_tail,
    xf, xft, xb, xbt, xg, xgt, wg, wu, wd, yf, yft, yb, ybt, hid_a, hid_b, tail_rows,
    w_local, w_send, w_recv, send_m, send_t, recv_m, recv_t, back_m, back_t, home_m, home_t,
):
    me = lax.axis_index("expert")
    x_lo = me // RING
    z = lax.rem(me, RING)
    block = z // SPLIT
    place = lax.rem(z, SPLIT)
    computing = jnp.logical_and(place >= 1, place <= 2)
    peer = me + 3 - 2 * place
    inner = jnp.where(place == 0, me + 1, me - 1)

    barrier = pltpu.get_barrier_semaphore()

    def greet(expert, carry):
        dest, _ = way(block, place, expert)

        @pl.when(dest != me)
        def _():
            pl.semaphore_signal(barrier, inc=1, device_id={"expert": dest}, device_id_type=MESH)

        return carry

    lax.fori_loop(0, EXPERTS, greet, 0)

    @pl.when(computing)
    def _():
        def greet_source(slot, carry):
            source = origin(block, place, slot)

            @pl.when(source != me)
            def _():
                pl.semaphore_signal(
                    barrier, inc=1, device_id={"expert": source}, device_id_type=MESH
                )

            return carry

        lax.fori_loop(0, SOURCES, greet_source, 0)
        pl.semaphore_signal(barrier, inc=1, device_id={"expert": peer}, device_id_type=MESH)
        pl.semaphore_wait(barrier, EXPERTS - 1 + SOURCES - 1 + 1)

    @pl.when(jnp.logical_not(computing))
    def _():
        pl.semaphore_wait(barrier, EXPERTS)

    weights = ((wg_in, wg), (wu_in, wu), (wd_in, wd))

    def share_rows(share):
        return pl.ds(pl.multiple_of(share * UNITS, UNITS), UNITS)

    def weight_copy(kind, source, share, where, device, passed):
        return pltpu.make_async_remote_copy(
            src_ref=source,
            dst_ref=weights[kind][1].at[share_rows(share)],
            send_sem=w_send.at[passed, kind],
            recv_sem=w_recv.at[where, kind],
            device_id={"expert": device},
            device_id_type=MESH,
        )

    for kind in range(3):
        own = weights[kind][0]

        @pl.when(computing)
        def _():
            weight_copy(kind, own, place, 0, peer, 0).start()
            pltpu.make_async_copy(own, weights[kind][1].at[share_rows(place)], w_local.at[kind]).start()

        @pl.when(jnp.logical_not(computing))
        def _():
            weight_copy(kind, own, place, 1, inner, 0).start()

    streams = (
        (f_main, f_tail, xf, xft),
        (b_main, b_tail, xb, xbt),
        (g_main, g_tail, xg, xgt),
    )

    def main_rows(index):
        return pl.ds(pl.multiple_of(index * MAIN, MAIN), MAIN)

    def send_stream(stream):
        main_in, tail_in, main_there, tail_there = streams[stream]

        def body(expert, carry):
            dest, kind = way(block, place, expert)
            slot = x_lo * 8 + kind
            pieces = (
                (main_in.at[main_rows(expert)], main_there.at[main_rows(slot)], send_m, recv_m),
                (tail_in.at[expert], tail_there.at[slot], send_t, recv_t),
            )
            for source, target, sent, got in pieces:

                @pl.when(dest == me)
                def _():
                    pltpu.make_async_copy(source, target, got.at[stream, slot]).start()

                @pl.when(dest != me)
                def _():
                    pltpu.make_async_remote_copy(
                        src_ref=source,
                        dst_ref=target,
                        send_sem=sent.at[stream, expert],
                        recv_sem=got.at[stream, slot],
                        device_id={"expert": dest},
                        device_id_type=MESH,
                    ).start()

            return carry

        lax.fori_loop(0, EXPERTS, body, 0)

    for stream in range(3):
        send_stream(stream)

    def wait_stream(stream):
        main_in, tail_in, main_there, tail_there = streams[stream]

        def body(slot, carry):
            pltpu.make_async_copy(
                main_in.at[main_rows(0)], main_there.at[main_rows(slot)], recv_m.at[stream, slot]
            ).wait()
            pltpu.make_async_copy(
                tail_in.at[0], tail_there.at[slot], recv_t.at[stream, slot]
            ).wait()
            return carry

        lax.fori_loop(0, SOURCES, body, 0)
        for slot in range(SOURCES):
            tail_rows[pl.ds(slot * TAIL, TAIL), :] = tail_there[slot].astype(jnp.float32)
        main_there[pl.ds(FIRST_TAIL, SOURCES * TAIL), :] = tail_rows[...].astype(jnp.bfloat16)

    def send_back(which, main_here, tail_here, main_home, tail_home):
        def body(slot, carry):
            source = origin(block, place, slot)
            expert = x_lo * BLOCKS + block
            pieces = (
                (main_here.at[main_rows(slot)], main_home.at[main_rows(expert)], back_m, home_m),
                (tail_here.at[slot], tail_home.at[expert], back_t, home_t),
            )
            for here, target, sent, got in pieces:

                @pl.when(source == me)
                def _():
                    pltpu.make_async_copy(here, target, got.at[which, expert]).start()

                @pl.when(source != me)
                def _():
                    pltpu.make_async_remote_copy(
                        src_ref=here,
                        dst_ref=target,
                        send_sem=sent.at[which, slot],
                        recv_sem=got.at[which, expert],
                        device_id={"expert": source},
                        device_id_type=MESH,
                    ).start()

            return carry

        lax.fori_loop(0, SOURCES, body, 0)

    def cols(step):
        return pl.ds(pl.multiple_of(step * TILE, TILE), TILE)

    def put_result(main_here, step, value):
        main_here[:, cols(step)] = value[:FIRST_TAIL].astype(jnp.bfloat16)
        tail_rows[:, cols(step)] = value[FIRST_TAIL:]

    def put_tails(tail_here):
        for slot in range(SOURCES):
            tail_here[slot] = tail_rows[pl.ds(slot * TAIL, TAIL), :].astype(jnp.bfloat16)

    def dot_nt(left, right):
        return lax.dot_general(left, right, NT, preferred_element_type=jnp.float32)

    def dot_nn(left, right):
        return jnp.dot(left, right, preferred_element_type=jnp.float32)

    @pl.when(computing)
    def _():
        outer_share = jnp.where(place == 1, 0, 3)
        for kind in range(3):
            held = weights[kind][1].at[share_rows(outer_share)]
            weight_copy(kind, held, outer_share, 1, inner, 0).wait_recv()
            weight_copy(kind, held, outer_share, 2, peer, 1).start()
        for kind in range(3):
            own = weights[kind][0]
            held = weights[kind][1].at[share_rows(place)]
            pltpu.make_async_copy(own, held, w_local.at[kind]).wait()
            far = weights[kind][1].at[share_rows(3 - place)]
            weight_copy(kind, far, 3 - place, 0, peer, 0).wait_recv()
            farther = weights[kind][1].at[share_rows(3 - outer_share)]
            weight_copy(kind, farther, 3 - outer_share, 2, peer, 1).wait_recv()

        wait_stream(0)

        def forward_hidden(step, carry):
            gate_pre = dot_nt(xf[...], wg[cols(step), :])
            up_pre = dot_nt(xf[...], wu[cols(step), :])
            hid_a[:, cols(step)] = (gate_pre * jax.nn.sigmoid(gate_pre) * up_pre).astype(
                jnp.bfloat16
            )
            return carry

        lax.fori_loop(0, WIDE // TILE, forward_hidden, 0)

        def forward_out(step, carry):
            put_result(yf, step, dot_nn(hid_a[...], wd[:, cols(step)]))
            return carry

        lax.fori_loop(0, D // TILE, forward_out, 0)
        put_tails(yft)
        send_back(0, yf, yft, of_main, of_tail)

        wait_stream(1)
        wait_stream(2)

        def backward_hidden(step, carry):
            gate_pre = dot_nt(xb[...], wg[cols(step), :])
            up_pre = dot_nt(xb[...], wu[cols(step), :])
            d_hidden = dot_nt(xg[...], wd[cols(step), :])
            sigma = jax.nn.sigmoid(gate_pre)
            hid_a[:, cols(step)] = (
                d_hidden * up_pre * (sigma * (1.0 + gate_pre * (1.0 - sigma)))
            ).astype(jnp.bfloat16)
            hid_b[:, cols(step)] = (d_hidden * (gate_pre * sigma)).astype(jnp.bfloat16)
            return carry

        lax.fori_loop(0, WIDE // TILE, backward_hidden, 0)

        def backward_out(step, carry):
            value = dot_nn(hid_a[...], wg[:, cols(step)]) + dot_nn(hid_b[...], wu[:, cols(step)])
            put_result(yb, step, value)
            return carry

        lax.fori_loop(0, D // TILE, backward_out, 0)
        put_tails(ybt)
        send_back(1, yb, ybt, ob_main, ob_tail)

    homes = ((yf, yft, of_main, of_tail), (yb, ybt, ob_main, ob_tail))
    for which in range(2):
        main_here, tail_here, main_home, tail_home = homes[which]

        def home(expert, carry):
            pltpu.make_async_copy(
                main_here.at[main_rows(0)], main_home.at[main_rows(expert)], home_m.at[which, expert]
            ).wait()
            pltpu.make_async_copy(
                tail_here.at[0], tail_home.at[expert], home_t.at[which, expert]
            ).wait()
            return carry

        lax.fori_loop(0, EXPERTS, home, 0)

    for stream in range(3):
        main_in, tail_in, main_there, tail_there = streams[stream]

        def left(expert, carry):
            dest, _ = way(block, place, expert)

            @pl.when(dest != me)
            def _():
                pltpu.make_async_copy(
                    main_in.at[main_rows(expert)], main_there.at[main_rows(0)],
                    send_m.at[stream, expert],
                ).wait()
                pltpu.make_async_copy(
                    tail_in.at[expert], tail_there.at[0], send_t.at[stream, expert]
                ).wait()

            return carry

        lax.fori_loop(0, EXPERTS, left, 0)

    for kind in range(3):
        weight_copy(kind, weights[kind][0], place, 0, inner, 0).wait_send()

    @pl.when(computing)
    def _():
        for kind in range(3):
            weight_copy(kind, weights[kind][0], place, 2, peer, 1).wait_send()
        for which in range(2):
            main_here, tail_here, main_home, tail_home = homes[which]

            def gone(slot, carry):
                source = origin(block, place, slot)

                @pl.when(source != me)
                def _():
                    pltpu.make_async_copy(
                        main_here.at[main_rows(slot)], main_home.at[main_rows(0)],
                        back_m.at[which, slot],
                    ).wait()
                    pltpu.make_async_copy(
                        tail_here.at[slot], tail_home.at[0], back_t.at[which, slot]
                    ).wait()

                return carry

            lax.fori_loop(0, SOURCES, gone, 0)


def run_experts(main_f, tail_f, main_b, tail_b, main_g, tail_g, gate_w, up_w, down_w):
    bf16 = jnp.bfloat16
    vmem = pl.BlockSpec(memory_space=pltpu.VMEM)
    dma = pltpu.SemaphoreType.DMA
    rows_in = pltpu.VMEM((ROWS, D), bf16)
    tails_in = pltpu.VMEM((SOURCES, TAIL, D), bf16)
    weight = pltpu.VMEM((WIDE, D), bf16)
    main_out = pltpu.VMEM((FIRST_TAIL, D), bf16)
    home_main = jax.ShapeDtypeStruct((EXPERTS * MAIN, D), bf16)
    home_tail = jax.ShapeDtypeStruct((EXPERTS, TAIL, D), bf16)
    return pl.pallas_call(
        expert_kernel,
        out_shape=(home_main, home_tail, home_main, home_tail),
        in_specs=[vmem] * 9,
        out_specs=(vmem,) * 4,
        scratch_shapes=[
            rows_in, tails_in, rows_in, tails_in, rows_in, tails_in,
            weight, weight, weight,
            main_out, tails_in, main_out, tails_in,
            pltpu.VMEM((ROWS, WIDE), bf16), pltpu.VMEM((ROWS, WIDE), bf16),
            pltpu.VMEM((SOURCES * TAIL, D), jnp.float32),
            dma((3,)), dma((2, 3)), dma((3, 3)),
            dma((3, EXPERTS)), dma((3, EXPERTS)), dma((3, SOURCES)), dma((3, SOURCES)),
            dma((2, SOURCES)), dma((2, SOURCES)), dma((2, EXPERTS)), dma((2, EXPERTS)),
        ],
        compiler_params=pltpu.CompilerParams(
            collective_id=0, has_side_effects=True, vmem_limit_bytes=48 * 1024 * 1024
        ),
        name="experts",
    )(main_f, tail_f, main_b, tail_b, main_g, tail_g, gate_w, up_w, down_w)


def split_rows(packed):
    main = packed[: EXPERTS * MAIN]
    return main, packed[EXPERTS * MAIN :].reshape(EXPERTS, TAIL, D)


def brought_home(chooser, main, tail, gates):
    rows = jnp.concatenate([main, tail.reshape(EXPERTS * TAIL, D)], axis=0)
    picked = lax.dot_general(
        chooser, rows, (((0,), (0,)), ((), ())), preferred_element_type=jnp.float32
    )
    return picked * gates


def per_device(
    act_in,
    saved_in,
    grad_in,
    norm_gain,
    w_gate,
    w_up,
    w_down,
    routes_fwd,
    gates_fwd,
    routes_bwd,
    gates_bwd,
):
    gain_row = norm_gain[0]
    incoming = passed_along(act_in, "section", 1)[0]
    upstream = passed_along(grad_in, "section", -1)[0]
    n_fwd = normalize(incoming, gain_row)[0].astype(jnp.bfloat16)
    values_b, inv_scale = normalize(saved_in[0], gain_row)
    n_bwd = values_b.astype(jnp.bfloat16)
    chooser_f = slot_chooser(routes_fwd[0])
    chooser_b = slot_chooser(routes_bwd[0])

    def packed(chooser, values):
        return split_rows(
            jnp.dot(chooser, values, preferred_element_type=jnp.float32).astype(jnp.bfloat16)
        )

    main_f, tail_f = packed(chooser_f, n_fwd)
    main_b, tail_b = packed(chooser_b, n_bwd)
    main_g, tail_g = packed(chooser_b, upstream)
    f_main, f_tail, b_main, b_tail = run_experts(
        main_f, tail_f, main_b, tail_b, main_g, tail_g, w_gate[0].T, w_up[0].T, w_down[0]
    )
    mixed = brought_home(chooser_f, f_main, f_tail, gates_fwd[0])
    act_out = (incoming.astype(jnp.float32) + mixed).astype(jnp.bfloat16)
    d_norm = brought_home(chooser_b, b_main, b_tail, gates_bwd[0])
    scaled = d_norm * gain_row
    base = saved_in[0].astype(jnp.float32)
    d_input = inv_scale * (
        scaled - base * inv_scale * inv_scale * jnp.mean(scaled * base, axis=-1, keepdims=True)
    )
    grad_out = (upstream.astype(jnp.float32) + d_input).astype(jnp.bfloat16)
    return (act_out[None], grad_out[None])


def solution(mesh):
    in_specs = (
        P("section", "expert", None),
        P("section", "expert", None),
        P("section", "expert", None),
        P("section", None),
        P("section", None, "expert"),
        P("section", None, "expert"),
        P("section", "expert", None),
        P("section", "expert", None),
        P("section", "expert", None),
        P("section", "expert", None),
        P("section", "expert", None),
    )
    out_specs = (P("section", "expert", None), P("section", "expert", None))
    return jax.shard_map(
        per_device, mesh=mesh, in_specs=in_specs, out_specs=out_specs, check_vma=False
    )
```

```python
import jax
import jax.numpy as jnp
from jax import lax
from jax.experimental import pallas as pl
from jax.experimental.pallas import tpu as pltpu
from jax.sharding import PartitionSpec as P

MESH = pl.DeviceIdType.MESH

SPLIT = 4
EXPERTS = 8
D = 2048
TOK = 128
UNITS = 192
WIDE = UNITS * SPLIT
MAIN = 16
TAIL = 2
PACKED = EXPERTS * (MAIN + TAIL)
EDGE_SLOTS = 14
SLOTS = 18
FIRST_TAIL = SLOTS * MAIN
TAIL_ROWS = SLOTS * TAIL
ROWS = 336
RING = 16
BLOCKS = RING // SPLIT
TILE = 256

norm_eps = 1e-06

NT = (((1,), (1,)), ((), ()))


def way(block, place, there):
    apart = lax.rem(there - block + BLOCKS, BLOCKS)
    low = place < 2
    to_edge = jnp.logical_or(
        apart == 1,
        jnp.logical_or(
            jnp.logical_and(apart == 2, place >= 2), jnp.logical_and(apart == 0, place == 0)
        ),
    )
    kind = jnp.where(
        apart == 0,
        jnp.where(place == 0, 6, 5 + place),
        jnp.where(apart == 2, jnp.where(low, 4 + place, 2 + place), place),
    )
    return jnp.where(to_edge, 0, 2), kind


def origin(block, place, slot):
    edge = place == 0
    stride = jnp.where(edge, EDGE_SLOTS // 2, SLOTS // 2)
    source_x = jnp.where(slot >= stride, 1, 0)
    kind = slot - source_x * stride
    apart = jnp.where(kind < 4, jnp.where(edge, 3, 1), jnp.where(kind < 6, 2, 0))
    source_place = jnp.where(
        kind < 4,
        kind,
        jnp.where(
            kind < 6,
            jnp.where(edge, kind - 2, kind - 4),
            jnp.where(edge, 0, kind - 5),
        ),
    )
    return source_x, lax.rem(block + apart, BLOCKS), source_place


def relay_kernel(
    act_in, saved_in, grad_in, gain, wg_in, wu_in, wd_in, routes_f, gates_f, routes_b, gates_b,
    act_out, grad_out,
    x_new, dy, f_main, f_tail, b_main, b_tail, g_main, g_tail,
    home_f, home_ft, home_b, home_bt, scaled,
    xf, xft, xb, xbt, xg, xgt, wg, wu, wd, yf, yft, yb, ybt, hid_a, hid_b, tail_rows, own_tails,
    hop_send, hop_recv, w_local, w_send, w_recv,
    send_m, send_t, recv_m, recv_t, back_m, back_t, home_m, home_ts,
):
    me = lax.axis_index("expert")
    section = lax.axis_index("section")
    sections = lax.axis_size("section")
    after = lax.rem(section + 1, sections)
    ahead = lax.rem(section + sections - 1, sections)
    mirrored = lax.rem(section, 2) == 1
    x_lo = me // RING
    z = lax.rem(me, RING)
    turned = jnp.where(mirrored, RING - 1 - z, z)
    block = turned // SPLIT
    place = lax.rem(turned, SPLIT)
    edge = place == 0
    middle = place == 2
    computing = jnp.logical_or(edge, middle)
    slots = jnp.where(edge, EDGE_SLOTS, SLOTS)

    def device(x, its_block, its_place):
        along = its_block * SPLIT + its_place
        return x * RING + jnp.where(mirrored, RING - 1 - along, along)

    def neighbour(its_place):
        return device(x_lo, block, its_place)

    def expert_row(x, its_block):
        return x * BLOCKS + jnp.where(mirrored, BLOCKS - 1 - its_block, its_block)

    own_expert = expert_row(x_lo, block)

    def target_of(number):
        x = number // BLOCKS
        there = lax.rem(number, BLOCKS)
        member, kind = way(block, place, there)
        slot = x_lo * jnp.where(member == 0, EDGE_SLOTS // 2, SLOTS // 2) + kind
        return device(x, there, member), slot, expert_row(x, there)

    def source_of(slot):
        return device(*origin(block, place, slot))

    barrier = pltpu.get_barrier_semaphore()

    def signal(name, index):
        pl.semaphore_signal(barrier, inc=1, device_id={name: index}, device_id_type=MESH)

    signal("section", after)
    signal("section", ahead)

    def greet(number, carry):
        dest, _, _ = target_of(number)

        @pl.when(dest != me)
        def _():
            signal("expert", dest)

        return carry

    lax.fori_loop(0, EXPERTS, greet, 0)

    @pl.when(computing)
    def _():
        def greet_source(slot, carry):
            source = source_of(slot)

            @pl.when(source != me)
            def _():
                signal("expert", source)

            return carry

        lax.fori_loop(0, slots, greet_source, 0)

    @pl.when(edge)
    def _():
        signal("expert", neighbour(1))
        signal("expert", neighbour(2))

    @pl.when(jnp.logical_or(place == 1, middle))
    def _():
        signal("expert", neighbour(0))

    def one_hots(routes):
        down = lax.broadcasted_iota(jnp.int32, (TOK, TOK), 0)
        across = lax.broadcasted_iota(jnp.int32, (TOK, TOK), 1)
        row = routes[...].astype(jnp.float32)
        rows = jnp.broadcast_to(row, (TOK, TOK))
        column = jnp.sum(jnp.where(down == across, rows, 0.0), axis=1, keepdims=True)
        same = rows == column
        slot_row = jnp.sum(jnp.where(jnp.logical_and(same, down < across), 1.0, 0.0), axis=0, keepdims=True)
        slot_column = jnp.sum(jnp.where(jnp.logical_and(same, across < down), 1.0, 0.0), axis=1, keepdims=True)

        def packed_row(expert, slot):
            return jnp.where(
                slot < MAIN, expert * MAIN + slot, EXPERTS * MAIN + expert * TAIL + slot - MAIN
            ).astype(jnp.int32)

        pick_in = lax.broadcasted_iota(jnp.int32, (PACKED, TOK), 0) == packed_row(row, slot_row)
        pick_out = lax.broadcasted_iota(jnp.int32, (TOK, PACKED), 1) == packed_row(column, slot_column)
        return (
            jnp.where(pick_in, 1.0, 0.0).astype(jnp.bfloat16),
            jnp.where(pick_out, 1.0, 0.0).astype(jnp.bfloat16),
        )

    def as_column(row_ref):
        down = lax.broadcasted_iota(jnp.int32, (TOK, TOK), 0)
        across = lax.broadcasted_iota(jnp.int32, (TOK, TOK), 1)
        rows = jnp.broadcast_to(row_ref[...], (TOK, TOK))
        return jnp.sum(jnp.where(down == across, rows, 0.0), axis=1, keepdims=True)

    def inverse_scale(rows):
        values = rows[...].astype(jnp.float32)
        return lax.rsqrt(jnp.mean(values * values, axis=-1, keepdims=True) + norm_eps)

    def static_cols(step):
        return slice(step * TILE, (step + 1) * TILE)

    def pack(chooser, rows, inv_scale, main, tail):
        for step in range(D // TILE):
            part = rows[:, static_cols(step)]
            if inv_scale is not None:
                part = (part.astype(jnp.float32) * inv_scale * gain[:, static_cols(step)]).astype(
                    jnp.bfloat16
                )
            value = jnp.dot(chooser, part, preferred_element_type=jnp.float32)
            main[:, static_cols(step)] = value[: EXPERTS * MAIN].astype(jnp.bfloat16)
            own_tails[:, static_cols(step)] = value[EXPERTS * MAIN :]
        for expert in range(EXPERTS):
            tail[expert] = own_tails[expert * TAIL : (expert + 1) * TAIL, :].astype(jnp.bfloat16)

    chooser_b, chosen_b = one_hots(routes_b)
    inv_b = inverse_scale(saved_in)
    pack(chooser_b, saved_in, inv_b, b_main, b_tail)

    pl.semaphore_wait(
        barrier,
        jnp.where(edge, 24, jnp.where(middle, 27, jnp.where(place == 1, 11, 10))),
    )

    weights = ((wg_in, wg), (wu_in, wu), (wd_in, wd))

    def share_rows(share):
        return pl.ds(pl.multiple_of(share * UNITS, UNITS), UNITS)

    def weight_copy(kind, source, share, sent, dest):
        return pltpu.make_async_remote_copy(
            src_ref=source,
            dst_ref=weights[kind][1].at[share_rows(share)],
            send_sem=w_send.at[sent, kind],
            recv_sem=w_recv.at[share, kind],
            device_id={"expert": dest},
            device_id_type=MESH,
        )

    def hop(source, target, number, there):
        return pltpu.make_async_remote_copy(
            src_ref=source,
            dst_ref=target,
            send_sem=hop_send.at[number],
            recv_sem=hop_recv.at[number],
            device_id={"section": there},
            device_id_type=MESH,
        )

    hop_act = hop(act_in, x_new, 0, after)
    hop_grad = hop(grad_in, dy, 1, ahead)
    hop_act.start()
    hop_grad.start()

    for kind in range(3):
        own = weights[kind][0]

        @pl.when(edge)
        def _():
            weight_copy(kind, own, 0, 0, neighbour(2)).start()

        @pl.when(place == 1)
        def _():
            weight_copy(kind, own, 1, 0, neighbour(0)).start()
            weight_copy(kind, own, 1, 1, neighbour(2)).start()

        @pl.when(middle)
        def _():
            weight_copy(kind, own, 2, 0, neighbour(0)).start()

        @pl.when(place == 3)
        def _():
            weight_copy(kind, own, 3, 0, neighbour(2)).start()

        @pl.when(computing)
        def _():
            pltpu.make_async_copy(
                own, weights[kind][1].at[share_rows(place)], w_local.at[kind]
            ).start()

    streams = (
        (f_main, f_tail, xf, xft),
        (b_main, b_tail, xb, xbt),
        (g_main, g_tail, xg, xgt),
    )

    def main_rows(index):
        return pl.ds(pl.multiple_of(index * MAIN, MAIN), MAIN)

    def send_stream(stream):
        main_in, tail_in, main_there, tail_there = streams[stream]

        def body(number, carry):
            dest, slot, expert = target_of(number)
            pieces = (
                (main_in.at[main_rows(expert)], main_there.at[main_rows(slot)], send_m, recv_m),
                (tail_in.at[expert], tail_there.at[slot], send_t, recv_t),
            )
            for source, target, sent, got in pieces:

                @pl.when(dest == me)
                def _():
                    pltpu.make_async_copy(source, target, got.at[stream, slot]).start()

                @pl.when(dest != me)
                def _():
                    pltpu.make_async_remote_copy(
                        src_ref=source,
                        dst_ref=target,
                        send_sem=sent.at[stream, number],
                        recv_sem=got.at[stream, slot],
                        device_id={"expert": dest},
                        device_id_type=MESH,
                    ).start()

            return carry

        lax.fori_loop(0, EXPERTS, body, 0)

    send_stream(1)

    chooser_f, chosen_f = one_hots(routes_f)
    hop_act.wait_recv()
    pack(chooser_f, x_new, inverse_scale(x_new), f_main, f_tail)
    send_stream(0)

    hop_grad.wait_recv()
    pack(chooser_b, dy, None, g_main, g_tail)
    send_stream(2)

    def wait_stream(stream):
        main_in, tail_in, main_there, tail_there = streams[stream]

        def body(slot, carry):
            pltpu.make_async_copy(
                main_in.at[main_rows(0)], main_there.at[main_rows(slot)], recv_m.at[stream, slot]
            ).wait()
            pltpu.make_async_copy(
                tail_in.at[0], tail_there.at[slot], recv_t.at[stream, slot]
            ).wait()
            return carry

        lax.fori_loop(0, slots, body, 0)
        for slot in range(SLOTS):
            tail_rows[slot * TAIL : (slot + 1) * TAIL, :] = tail_there[slot].astype(jnp.float32)
        main_there[FIRST_TAIL:ROWS, :] = tail_rows[...].astype(jnp.bfloat16)

    def send_back(which, main_here, tail_here, main_home, tail_home):
        def body(slot, carry):
            source = source_of(slot)
            pieces = (
                (main_here.at[main_rows(slot)], main_home.at[main_rows(own_expert)], back_m, home_m),
                (tail_here.at[slot], tail_home.at[own_expert], back_t, home_ts),
            )
            for here, target, sent, got in pieces:

                @pl.when(source == me)
                def _():
                    pltpu.make_async_copy(here, target, got.at[which, own_expert]).start()

                @pl.when(source != me)
                def _():
                    pltpu.make_async_remote_copy(
                        src_ref=here,
                        dst_ref=target,
                        send_sem=sent.at[which, slot],
                        recv_sem=got.at[which, own_expert],
                        device_id={"expert": source},
                        device_id_type=MESH,
                    ).start()

            return carry

        lax.fori_loop(0, slots, body, 0)

    def cols(step):
        return pl.ds(pl.multiple_of(step * TILE, TILE), TILE)

    def put_result(main_here, step, value):
        main_here[:, cols(step)] = value[:FIRST_TAIL].astype(jnp.bfloat16)
        tail_rows[:, cols(step)] = value[FIRST_TAIL:]

    def put_tails(tail_here):
        for slot in range(SLOTS):
            tail_here[slot] = tail_rows[slot * TAIL : (slot + 1) * TAIL, :].astype(jnp.bfloat16)

    def dot_nt(left, right):
        return lax.dot_general(left, right, NT, preferred_element_type=jnp.float32)

    def dot_nn(left, right):
        return jnp.dot(left, right, preferred_element_type=jnp.float32)

    @pl.when(middle)
    def _():
        for kind in range(3):
            held = weights[kind][1].at[share_rows(3)]
            weight_copy(kind, held, 3, 0, neighbour(0)).wait_recv()
            weight_copy(kind, held, 3, 1, neighbour(0)).start()

    @pl.when(computing)
    def _():
        for kind in range(3):
            own = weights[kind][0]
            held = weights[kind][1].at[share_rows(place)]
            pltpu.make_async_copy(own, held, w_local.at[kind]).wait()
            weight_copy(kind, held, 1, 0, neighbour(0)).wait_recv()
            weight_copy(kind, held, jnp.where(edge, 2, 0), 0, neighbour(0)).wait_recv()

        @pl.when(edge)
        def _():
            for kind in range(3):
                held = weights[kind][1].at[share_rows(3)]
                weight_copy(kind, held, 3, 0, neighbour(0)).wait_recv()

        wait_stream(0)

        def forward_hidden(step, carry):
            gate_pre = dot_nt(xf[...], wg[cols(step), :])
            up_pre = dot_nt(xf[...], wu[cols(step), :])
            hid_a[:, cols(step)] = (gate_pre * jax.nn.sigmoid(gate_pre) * up_pre).astype(
                jnp.bfloat16
            )
            return carry

        lax.fori_loop(0, WIDE // TILE, forward_hidden, 0)

        def forward_out(step, carry):
            put_result(yf, step, dot_nn(hid_a[...], wd[:, cols(step)]))
            return carry

        lax.fori_loop(0, D // TILE, forward_out, 0)
        put_tails(yft)
        send_back(0, yf, yft, home_f, home_ft)

        wait_stream(1)
        wait_stream(2)

        def backward_hidden(step, carry):
            gate_pre = dot_nt(xb[...], wg[cols(step), :])
            up_pre = dot_nt(xb[...], wu[cols(step), :])
            d_hidden = dot_nt(xg[...], wd[cols(step), :])
            sigma = jax.nn.sigmoid(gate_pre)
            hid_a[:, cols(step)] = (
                d_hidden * up_pre * (sigma * (1.0 + gate_pre * (1.0 - sigma)))
            ).astype(jnp.bfloat16)
            hid_b[:, cols(step)] = (d_hidden * (gate_pre * sigma)).astype(jnp.bfloat16)
            return carry

        lax.fori_loop(0, WIDE // TILE, backward_hidden, 0)

        def backward_out(step, carry):
            value = dot_nn(hid_a[...], wg[:, cols(step)]) + dot_nn(hid_b[...], wu[:, cols(step)])
            put_result(yb, step, value)
            return carry

        lax.fori_loop(0, D // TILE, backward_out, 0)
        put_tails(ybt)
        send_back(1, yb, ybt, home_b, home_bt)

    homes = ((yf, yft, home_f, home_ft), (yb, ybt, home_b, home_bt))

    def wait_home(which):
        main_here, tail_here, main_home, tail_home = homes[which]

        def body(expert, carry):
            pltpu.make_async_copy(
                main_here.at[main_rows(0)], main_home.at[main_rows(expert)], home_m.at[which, expert]
            ).wait()
            pltpu.make_async_copy(
                tail_here.at[0], tail_home.at[expert], home_ts.at[which, expert]
            ).wait()
            return carry

        lax.fori_loop(0, EXPERTS, body, 0)
        for expert in range(EXPERTS):
            own_tails[expert * TAIL : (expert + 1) * TAIL, :] = tail_home[expert].astype(jnp.float32)
        main_home[EXPERTS * MAIN :, :] = own_tails[...].astype(jnp.bfloat16)

    wait_home(0)
    gate_f = as_column(gates_f)
    for step in range(D // TILE):
        part = static_cols(step)
        mixed = dot_nn(chosen_f, home_f[:, part]) * gate_f
        act_out[:, part] = (x_new[:, part].astype(jnp.float32) + mixed).astype(jnp.bfloat16)

    wait_home(1)
    gate_b = as_column(gates_b)
    total = jnp.zeros((TOK, 1), jnp.float32)
    for step in range(D // TILE):
        part = static_cols(step)
        value = dot_nn(chosen_b, home_b[:, part]) * gate_b * gain[:, part]
        scaled[:, part] = value
        total = total + jnp.sum(
            value * saved_in[:, part].astype(jnp.float32), axis=-1, keepdims=True
        )
    inv_scale = inverse_scale(saved_in)
    fold = inv_scale * inv_scale * (total / D)
    for step in range(D // TILE):
        part = static_cols(step)
        d_input = inv_scale * (scaled[:, part] - saved_in[:, part].astype(jnp.float32) * fold)
        grad_out[:, part] = (dy[:, part].astype(jnp.float32) + d_input).astype(jnp.bfloat16)

    hop_act.wait_send()
    hop_grad.wait_send()

    for stream in range(3):
        main_in, tail_in, main_there, tail_there = streams[stream]

        def left(number, carry):
            dest, _, expert = target_of(number)

            @pl.when(dest != me)
            def _():
                pltpu.make_async_copy(
                    main_in.at[main_rows(expert)], main_there.at[main_rows(0)],
                    send_m.at[stream, number],
                ).wait()
                pltpu.make_async_copy(
                    tail_in.at[expert], tail_there.at[0], send_t.at[stream, number]
                ).wait()

            return carry

        lax.fori_loop(0, EXPERTS, left, 0)

    for kind in range(3):
        weight_copy(kind, weights[kind][0], 0, 0, neighbour(0)).wait_send()

    @pl.when(jnp.logical_or(place == 1, middle))
    def _():
        for kind in range(3):
            weight_copy(kind, weights[kind][0], 0, 1, neighbour(0)).wait_send()

    @pl.when(computing)
    def _():
        for which in range(2):
            main_here, tail_here, main_home, tail_home = homes[which]

            def gone(slot, carry):
                source = source_of(slot)

                @pl.when(source != me)
                def _():
                    pltpu.make_async_copy(
                        main_here.at[main_rows(slot)], main_home.at[main_rows(0)],
                        back_m.at[which, slot],
                    ).wait()
                    pltpu.make_async_copy(
                        tail_here.at[slot], tail_home.at[0], back_t.at[which, slot]
                    ).wait()

                return carry

            lax.fori_loop(0, slots, gone, 0)


def run_relay(*operands):
    bf16 = jnp.bfloat16
    vmem = pl.BlockSpec(memory_space=pltpu.VMEM)
    anywhere = pl.BlockSpec(memory_space=pl.ANY)
    dma = pltpu.SemaphoreType.DMA
    tokens = pltpu.VMEM((TOK, D), bf16)
    packed_main = pltpu.VMEM((EXPERTS * MAIN, D), bf16)
    packed_tail = pltpu.VMEM((EXPERTS, TAIL, D), bf16)
    home_main = pltpu.VMEM((PACKED, D), bf16)
    rows_in = pltpu.VMEM((ROWS, D), bf16)
    tails_in = pltpu.VMEM((SLOTS, TAIL, D), bf16)
    weight = pltpu.VMEM((WIDE, D), bf16)
    main_out = pltpu.VMEM((FIRST_TAIL, D), bf16)
    hidden = pltpu.VMEM((ROWS, WIDE), bf16)
    out = jax.ShapeDtypeStruct((TOK, D), bf16)
    return pl.pallas_call(
        relay_kernel,
        out_shape=(out, out),
        in_specs=[anywhere, vmem, anywhere, vmem, anywhere, anywhere, anywhere, vmem, vmem, vmem, vmem],
        out_specs=(vmem, vmem),
        scratch_shapes=[
            tokens, tokens, packed_main, packed_tail, packed_main, packed_tail, packed_main, packed_tail,
            home_main, packed_tail, home_main, packed_tail, pltpu.VMEM((TOK, D), jnp.float32),
            rows_in, tails_in, rows_in, tails_in, rows_in, tails_in,
            weight, weight, weight,
            main_out, tails_in, main_out, tails_in,
            hidden, hidden,
            pltpu.VMEM((ROWS - FIRST_TAIL, D), jnp.float32),
            pltpu.VMEM((EXPERTS * TAIL, D), jnp.float32),
            dma((2,)), dma((2,)), dma((3,)), dma((2, 3)), dma((SPLIT, 3)),
            dma((3, EXPERTS)), dma((3, EXPERTS)), dma((3, SLOTS)), dma((3, SLOTS)),
            dma((2, SLOTS)), dma((2, SLOTS)), dma((2, EXPERTS)), dma((2, EXPERTS)),
        ],
        compiler_params=pltpu.CompilerParams(
            collective_id=0, has_side_effects=True, vmem_limit_bytes=52 * 1024 * 1024
        ),
        name="relay",
    )(*operands)


def per_device(
    act_in,
    saved_in,
    grad_in,
    norm_gain,
    w_gate,
    w_up,
    w_down,
    routes_fwd,
    gates_fwd,
    routes_bwd,
    gates_bwd,
):
    act_out, grad_out = run_relay(
        act_in[0],
        saved_in[0],
        grad_in[0],
        norm_gain,
        w_gate[0].T,
        w_up[0].T,
        w_down[0],
        routes_fwd.reshape(1, TOK),
        gates_fwd.reshape(1, TOK),
        routes_bwd.reshape(1, TOK),
        gates_bwd.reshape(1, TOK),
    )
    return (act_out[None], grad_out[None])


def solution(mesh):
    in_specs = (
        P("section", "expert", None),
        P("section", "expert", None),
        P("section", "expert", None),
        P("section", None),
        P("section", None, "expert"),
        P("section", None, "expert"),
        P("section", "expert", None),
        P("section", "expert", None),
        P("section", "expert", None),
        P("section", "expert", None),
        P("section", "expert", None),
    )
    out_specs = (P("section", "expert", None), P("section", "expert", None))
    return jax.shard_map(
        per_device, mesh=mesh, in_specs=in_specs, out_specs=out_specs, check_vma=False
    )
```

```python
import jax
import jax.numpy as jnp
from jax import lax
from jax.experimental import pallas as pl
from jax.experimental.pallas import tpu as pltpu
from jax.sharding import PartitionSpec as P

MESH = pl.DeviceIdType.MESH

SPLIT = 4
EXPERTS = 8
D = 2048
TOK = 128
UNITS = 192
PIECES = 3
PIECE = UNITS // PIECES
WIDE = UNITS * SPLIT
MAIN = 16
TAIL = 2
PACKED = EXPERTS * (MAIN + TAIL)
SLOTS = 16
FIRST_TAIL = SLOTS * MAIN
ROWS = SLOTS * (MAIN + TAIL)
RING = 16
BLOCKS = RING // SPLIT
TILE = 256

norm_eps = 1e-06

NT = (((1,), (1,)), ((), ()))


def way(block, place, there):
    apart = lax.rem(there - block + BLOCKS, BLOCKS)
    first = place == 0
    to_edge = jnp.logical_or(
        apart == 1,
        jnp.logical_or(
            jnp.logical_and(apart == 2, place >= 1), jnp.logical_and(apart == 0, first)
        ),
    )
    kind = jnp.where(
        apart == 0,
        jnp.where(first, 7, 4 + place),
        jnp.where(apart == 2, jnp.where(first, 4, 3 + place), place),
    )
    return jnp.where(to_edge, 0, 1), kind


def origin(block, place, slot):
    edge = place == 0
    kind = lax.rem(slot, 8)
    opposite = jnp.where(edge, 6, 4)
    apart = jnp.where(kind < 4, jnp.where(edge, 3, 1), jnp.where(kind <= opposite, 2, 0))
    source_place = jnp.where(
        kind < 4,
        kind,
        jnp.where(edge, jnp.where(kind == 7, 0, kind - 3), kind - 4),
    )
    return slot // 8, lax.rem(block + apart, BLOCKS), source_place


def relay_kernel(
    act_in, saved_in, grad_in, gain, wg_in, wu_in, wd_in, routes_f, gates_f, routes_b, gates_b,
    act_out, grad_out,
    x_new, dy, f_main, f_tail, b_main, b_tail, g_main, g_tail,
    home_f, home_ft, home_b, home_bt, scaled,
    xf, xft, xb, xbt, xg, xgt, wg, wu, wd, yf, yft, yb, ybt, hid_a, hid_b, tail_rows, own_tails,
    hop_send, hop_recv, w_local, w_send, w_recv,
    send_m, send_t, recv_m, recv_t, back_m, back_t, home_m, home_ts,
):
    me = lax.axis_index("expert")
    section = lax.axis_index("section")
    sections = lax.axis_size("section")
    after = lax.rem(section + 1, sections)
    ahead = lax.rem(section + sections - 1, sections)
    mirrored = lax.rem(section, 2) == 1
    x_lo = me // RING
    z = lax.rem(me, RING)
    turned = jnp.where(mirrored, RING - 1 - z, z)
    block = turned // SPLIT
    place = lax.rem(turned, SPLIT)
    edge = place == 0
    middle = place == 1
    computing = place < 2

    def device(x, its_block, its_place):
        along = its_block * SPLIT + its_place
        return x * RING + jnp.where(mirrored, RING - 1 - along, along)

    def neighbour(its_place):
        return device(x_lo, block, its_place)

    def expert_row(x, its_block):
        return x * BLOCKS + jnp.where(mirrored, BLOCKS - 1 - its_block, its_block)

    own_expert = expert_row(x_lo, block)

    def target_of(number):
        x = number // BLOCKS
        there = lax.rem(number, BLOCKS)
        member, kind = way(block, place, there)
        slot = x_lo * (SLOTS // 2) + kind
        return device(x, there, member), slot, expert_row(x, there)

    def source_of(slot):
        return device(*origin(block, place, slot))

    barrier = pltpu.get_barrier_semaphore()

    def signal(name, index):
        pl.semaphore_signal(barrier, inc=1, device_id={name: index}, device_id_type=MESH)

    signal("section", after)
    signal("section", ahead)

    def greet(number, carry):
        dest, _, _ = target_of(number)

        @pl.when(dest != me)
        def _():
            signal("expert", dest)

        return carry

    lax.fori_loop(0, EXPERTS, greet, 0)

    @pl.when(computing)
    def _():
        def greet_source(slot, carry):
            source = source_of(slot)

            @pl.when(source != me)
            def _():
                signal("expert", source)

            return carry

        lax.fori_loop(0, SLOTS, greet_source, 0)
        signal("expert", neighbour(1 - place))

    pl.semaphore_wait(barrier, jnp.where(computing, 7 + 15 + 1 + 2, 8 + 2))

    weights = ((wg_in, wg), (wu_in, wu), (wd_in, wd))

    def share_rows(share):
        return pl.ds(pl.multiple_of(share * UNITS, UNITS), UNITS)

    def piece_rows(start):
        return pl.ds(pl.multiple_of(start, PIECE), PIECE)

    def weight_copy(kind, piece, share, sent, dest, passed=False):
        there = weights[kind][1].at[piece_rows(share * UNITS + piece * PIECE)]
        return pltpu.make_async_remote_copy(
            src_ref=there if passed else weights[kind][0].at[piece_rows(piece * PIECE)],
            dst_ref=there,
            send_sem=w_send.at[sent, kind, piece],
            recv_sem=w_recv.at[share, kind, piece],
            device_id={"expert": dest},
            device_id_type=MESH,
        )

    def each_piece(body):
        for kind in range(3):

            def step(piece, carry):
                body(kind, piece)
                return carry

            lax.fori_loop(0, PIECES, step, 0)

    def hop(source, target, number, there):
        return pltpu.make_async_remote_copy(
            src_ref=source,
            dst_ref=target,
            send_sem=hop_send.at[number],
            recv_sem=hop_recv.at[number],
            device_id={"section": there},
            device_id_type=MESH,
        )

    each_piece(
        lambda kind, piece: weight_copy(
            kind, piece, place, 0, neighbour(jnp.where(middle, 0, 1))
        ).start()
    )

    for kind in range(3):
        own = weights[kind][0]

        @pl.when(computing)
        def _():
            pltpu.make_async_copy(
                own, weights[kind][1].at[share_rows(place)], w_local.at[kind]
            ).start()

    hop_act = hop(act_in, x_new, 0, after)
    hop_grad = hop(grad_in, dy, 1, ahead)
    hop_act.start()
    hop_grad.start()

    def one_hots(routes):
        down = lax.broadcasted_iota(jnp.int32, (TOK, TOK), 0)
        across = lax.broadcasted_iota(jnp.int32, (TOK, TOK), 1)
        row = routes[...].astype(jnp.float32)
        rows = jnp.broadcast_to(row, (TOK, TOK))
        column = jnp.sum(jnp.where(down == across, rows, 0.0), axis=1, keepdims=True)
        same = rows == column
        slot_row = jnp.sum(jnp.where(jnp.logical_and(same, down < across), 1.0, 0.0), axis=0, keepdims=True)
        slot_column = jnp.sum(jnp.where(jnp.logical_and(same, across < down), 1.0, 0.0), axis=1, keepdims=True)

        def packed_row(expert, slot):
            return jnp.where(
                slot < MAIN, expert * MAIN + slot, EXPERTS * MAIN + expert * TAIL + slot - MAIN
            ).astype(jnp.int32)

        pick_in = lax.broadcasted_iota(jnp.int32, (PACKED, TOK), 0) == packed_row(row, slot_row)
        pick_out = lax.broadcasted_iota(jnp.int32, (TOK, PACKED), 1) == packed_row(column, slot_column)
        return (
            jnp.where(pick_in, 1.0, 0.0).astype(jnp.bfloat16),
            jnp.where(pick_out, 1.0, 0.0).astype(jnp.bfloat16),
        )

    def as_column(row_ref):
        down = lax.broadcasted_iota(jnp.int32, (TOK, TOK), 0)
        across = lax.broadcasted_iota(jnp.int32, (TOK, TOK), 1)
        rows = jnp.broadcast_to(row_ref[...], (TOK, TOK))
        return jnp.sum(jnp.where(down == across, rows, 0.0), axis=1, keepdims=True)

    def inverse_scale(rows):
        values = rows[...].astype(jnp.float32)
        return lax.rsqrt(jnp.mean(values * values, axis=-1, keepdims=True) + norm_eps)

    def static_cols(step):
        return slice(step * TILE, (step + 1) * TILE)

    def pack(chooser, rows, inv_scale, main, tail):
        for step in range(D // TILE):
            part = rows[:, static_cols(step)]
            if inv_scale is not None:
                part = (part.astype(jnp.float32) * inv_scale * gain[:, static_cols(step)]).astype(
                    jnp.bfloat16
                )
            value = jnp.dot(chooser, part, preferred_element_type=jnp.float32)
            main[:, static_cols(step)] = value[: EXPERTS * MAIN].astype(jnp.bfloat16)
            own_tails[:, static_cols(step)] = value[EXPERTS * MAIN :]
        for expert in range(EXPERTS):
            tail[expert] = own_tails[expert * TAIL : (expert + 1) * TAIL, :].astype(jnp.bfloat16)

    streams = (
        (f_main, f_tail, xf, xft),
        (b_main, b_tail, xb, xbt),
        (g_main, g_tail, xg, xgt),
    )

    def main_rows(index):
        return pl.ds(pl.multiple_of(index * MAIN, MAIN), MAIN)

    def send_stream(stream):
        main_in, tail_in, main_there, tail_there = streams[stream]

        def body(number, carry):
            dest, slot, expert = target_of(number)
            pieces = (
                (main_in.at[main_rows(expert)], main_there.at[main_rows(slot)], send_m, recv_m),
                (tail_in.at[expert], tail_there.at[slot], send_t, recv_t),
            )
            for source, target, sent, got in pieces:

                @pl.when(dest == me)
                def _():
                    pltpu.make_async_copy(source, target, got.at[stream, slot]).start()

                @pl.when(dest != me)
                def _():
                    pltpu.make_async_remote_copy(
                        src_ref=source,
                        dst_ref=target,
                        send_sem=sent.at[stream, number],
                        recv_sem=got.at[stream, slot],
                        device_id={"expert": dest},
                        device_id_type=MESH,
                    ).start()

            return carry

        lax.fori_loop(0, EXPERTS, body, 0)

    chooser_b, chosen_b = one_hots(routes_b)
    inv_b = inverse_scale(saved_in)
    pack(chooser_b, saved_in, inv_b, b_main, b_tail)
    send_stream(1)

    hop_grad.wait_recv()
    pack(chooser_b, dy, None, g_main, g_tail)
    send_stream(2)

    chooser_f, chosen_f = one_hots(routes_f)
    hop_act.wait_recv()
    pack(chooser_f, x_new, inverse_scale(x_new), f_main, f_tail)
    def wait_stream(stream):
        main_in, tail_in, main_there, tail_there = streams[stream]

        def body(slot, carry):
            pltpu.make_async_copy(
                main_in.at[main_rows(0)], main_there.at[main_rows(slot)], recv_m.at[stream, slot]
            ).wait()
            pltpu.make_async_copy(
                tail_in.at[0], tail_there.at[slot], recv_t.at[stream, slot]
            ).wait()
            return carry

        lax.fori_loop(0, SLOTS, body, 0)
        for slot in range(SLOTS):
            tail_rows[slot * TAIL : (slot + 1) * TAIL, :] = tail_there[slot].astype(jnp.float32)
        main_there[FIRST_TAIL:ROWS, :] = tail_rows[...].astype(jnp.bfloat16)

    def send_back(which, main_here, tail_here, main_home, tail_home):
        def body(slot, carry):
            source = source_of(slot)
            pieces = (
                (main_here.at[main_rows(slot)], main_home.at[main_rows(own_expert)], back_m, home_m),
                (tail_here.at[slot], tail_home.at[own_expert], back_t, home_ts),
            )
            for here, target, sent, got in pieces:

                @pl.when(source == me)
                def _():
                    pltpu.make_async_copy(here, target, got.at[which, own_expert]).start()

                @pl.when(source != me)
                def _():
                    pltpu.make_async_remote_copy(
                        src_ref=here,
                        dst_ref=target,
                        send_sem=sent.at[which, slot],
                        recv_sem=got.at[which, own_expert],
                        device_id={"expert": source},
                        device_id_type=MESH,
                    ).start()

            return carry

        lax.fori_loop(0, SLOTS, body, 0)

    def cols(step):
        return pl.ds(pl.multiple_of(step * TILE, TILE), TILE)

    def put_result(main_here, step, value):
        main_here[:, cols(step)] = value[:FIRST_TAIL].astype(jnp.bfloat16)
        tail_rows[:, cols(step)] = value[FIRST_TAIL:]

    def put_tails(tail_here):
        for slot in range(SLOTS):
            tail_here[slot] = tail_rows[slot * TAIL : (slot + 1) * TAIL, :].astype(jnp.bfloat16)

    def dot_nt(left, right):
        return lax.dot_general(left, right, NT, preferred_element_type=jnp.float32)

    def dot_nn(left, right):
        return jnp.dot(left, right, preferred_element_type=jnp.float32)

    @pl.when(middle)
    def _():
        def pass_on(kind, piece):
            for share in (2, 3):
                weight_copy(kind, piece, share, 0, neighbour(0)).wait_recv()
                weight_copy(kind, piece, share, share - 1, neighbour(0), True).start()

        each_piece(pass_on)

    @pl.when(computing)
    def _():
        for kind in range(3):
            own = weights[kind][0]
            held = weights[kind][1].at[share_rows(place)]
            pltpu.make_async_copy(own, held, w_local.at[kind]).wait()

        each_piece(
            lambda kind, piece: weight_copy(kind, piece, 1 - place, 0, neighbour(0)).wait_recv()
        )

        @pl.when(edge)
        def _():
            def arrived(kind, piece):
                for share in (2, 3):
                    weight_copy(kind, piece, share, 0, neighbour(0)).wait_recv()

            each_piece(arrived)

    @pl.when(jnp.logical_not(computing))
    def _():
        each_piece(lambda kind, piece: weight_copy(kind, piece, 0, 0, neighbour(0)).wait_send())

    send_stream(0)

    @pl.when(computing)
    def _():
        wait_stream(1)
        wait_stream(2)

        def backward_hidden(step, carry):
            gate_pre = dot_nt(xb[...], wg[cols(step), :])
            up_pre = dot_nt(xb[...], wu[cols(step), :])
            d_hidden = dot_nt(xg[...], wd[cols(step), :])
            sigma = jax.nn.sigmoid(gate_pre)
            hid_a[:, cols(step)] = (
                d_hidden * up_pre * (sigma * (1.0 + gate_pre * (1.0 - sigma)))
            ).astype(jnp.bfloat16)
            hid_b[:, cols(step)] = (d_hidden * (gate_pre * sigma)).astype(jnp.bfloat16)
            return carry

        lax.fori_loop(0, WIDE // TILE, backward_hidden, 0)

        def backward_out(step, carry):
            value = dot_nn(hid_a[...], wg[:, cols(step)]) + dot_nn(hid_b[...], wu[:, cols(step)])
            put_result(yb, step, value)
            return carry

        lax.fori_loop(0, D // TILE, backward_out, 0)
        put_tails(ybt)
        send_back(1, yb, ybt, home_b, home_bt)

        wait_stream(0)

        def forward_hidden(step, carry):
            gate_pre = dot_nt(xf[...], wg[cols(step), :])
            up_pre = dot_nt(xf[...], wu[cols(step), :])
            hid_a[:, cols(step)] = (gate_pre * jax.nn.sigmoid(gate_pre) * up_pre).astype(
                jnp.bfloat16
            )
            return carry

        lax.fori_loop(0, WIDE // TILE, forward_hidden, 0)

        def forward_out(step, carry):
            put_result(yf, step, dot_nn(hid_a[...], wd[:, cols(step)]))
            return carry

        lax.fori_loop(0, D // TILE, forward_out, 0)
        put_tails(yft)
        send_back(0, yf, yft, home_f, home_ft)

    homes = ((yf, yft, home_f, home_ft), (yb, ybt, home_b, home_bt))

    def wait_home(which):
        main_here, tail_here, main_home, tail_home = homes[which]

        def body(expert, carry):
            pltpu.make_async_copy(
                main_here.at[main_rows(0)], main_home.at[main_rows(expert)], home_m.at[which, expert]
            ).wait()
            pltpu.make_async_copy(
                tail_here.at[0], tail_home.at[expert], home_ts.at[which, expert]
            ).wait()
            return carry

        lax.fori_loop(0, EXPERTS, body, 0)
        for expert in range(EXPERTS):
            own_tails[expert * TAIL : (expert + 1) * TAIL, :] = tail_home[expert].astype(jnp.float32)
        main_home[EXPERTS * MAIN :, :] = own_tails[...].astype(jnp.bfloat16)

    wait_home(1)
    gate_b = as_column(gates_b)
    total = jnp.zeros((TOK, 1), jnp.float32)
    for step in range(D // TILE):
        part = static_cols(step)
        value = dot_nn(chosen_b, home_b[:, part]) * gate_b * gain[:, part]
        scaled[:, part] = value
        total = total + jnp.sum(
            value * saved_in[:, part].astype(jnp.float32), axis=-1, keepdims=True
        )
    inv_scale = inverse_scale(saved_in)
    fold = inv_scale * inv_scale * (total / D)
    for step in range(D // TILE):
        part = static_cols(step)
        d_input = inv_scale * (scaled[:, part] - saved_in[:, part].astype(jnp.float32) * fold)
        grad_out[:, part] = (dy[:, part].astype(jnp.float32) + d_input).astype(jnp.bfloat16)

    wait_home(0)
    gate_f = as_column(gates_f)
    for step in range(D // TILE):
        part = static_cols(step)
        mixed = dot_nn(chosen_f, home_f[:, part]) * gate_f
        act_out[:, part] = (x_new[:, part].astype(jnp.float32) + mixed).astype(jnp.bfloat16)

    hop_act.wait_send()
    hop_grad.wait_send()

    for stream in range(3):
        main_in, tail_in, main_there, tail_there = streams[stream]

        def left(number, carry):
            dest, _, expert = target_of(number)

            @pl.when(dest != me)
            def _():
                pltpu.make_async_copy(
                    main_in.at[main_rows(expert)], main_there.at[main_rows(0)],
                    send_m.at[stream, number],
                ).wait()
                pltpu.make_async_copy(
                    tail_in.at[expert], tail_there.at[0], send_t.at[stream, number]
                ).wait()

            return carry

        lax.fori_loop(0, EXPERTS, left, 0)

    @pl.when(computing)
    def _():
        each_piece(lambda kind, piece: weight_copy(kind, piece, 0, 0, neighbour(0)).wait_send())

    @pl.when(middle)
    def _():
        def passed_on(kind, piece):
            for sent in (1, 2):
                weight_copy(kind, piece, 0, sent, neighbour(0)).wait_send()

        each_piece(passed_on)

    @pl.when(computing)
    def _():
        for which in range(2):
            main_here, tail_here, main_home, tail_home = homes[which]

            def gone(slot, carry):
                source = source_of(slot)

                @pl.when(source != me)
                def _():
                    pltpu.make_async_copy(
                        main_here.at[main_rows(slot)], main_home.at[main_rows(0)],
                        back_m.at[which, slot],
                    ).wait()
                    pltpu.make_async_copy(
                        tail_here.at[slot], tail_home.at[0], back_t.at[which, slot]
                    ).wait()

                return carry

            lax.fori_loop(0, SLOTS, gone, 0)


def run_relay(*operands):
    bf16 = jnp.bfloat16
    vmem = pl.BlockSpec(memory_space=pltpu.VMEM)
    anywhere = pl.BlockSpec(memory_space=pl.ANY)
    dma = pltpu.SemaphoreType.DMA
    tokens = pltpu.VMEM((TOK, D), bf16)
    packed_main = pltpu.VMEM((EXPERTS * MAIN, D), bf16)
    packed_tail = pltpu.VMEM((EXPERTS, TAIL, D), bf16)
    home_main = pltpu.VMEM((PACKED, D), bf16)
    rows_in = pltpu.VMEM((ROWS, D), bf16)
    tails_in = pltpu.VMEM((SLOTS, TAIL, D), bf16)
    weight = pltpu.VMEM((WIDE, D), bf16)
    main_out = pltpu.VMEM((FIRST_TAIL, D), bf16)
    hidden = pltpu.VMEM((ROWS, WIDE), bf16)
    out = jax.ShapeDtypeStruct((TOK, D), bf16)
    return pl.pallas_call(
        relay_kernel,
        out_shape=(out, out),
        in_specs=[anywhere, vmem, anywhere, vmem, anywhere, anywhere, anywhere, vmem, vmem, vmem, vmem],
        out_specs=(vmem, vmem),
        scratch_shapes=[
            tokens, tokens, packed_main, packed_tail, packed_main, packed_tail, packed_main, packed_tail,
            home_main, packed_tail, home_main, packed_tail, pltpu.VMEM((TOK, D), jnp.float32),
            rows_in, tails_in, rows_in, tails_in, rows_in, tails_in,
            weight, weight, weight,
            main_out, tails_in, main_out, tails_in,
            hidden, hidden,
            pltpu.VMEM((ROWS - FIRST_TAIL, D), jnp.float32),
            pltpu.VMEM((EXPERTS * TAIL, D), jnp.float32),
            dma((2,)), dma((2,)), dma((3,)), dma((3, 3, PIECES)), dma((SPLIT, 3, PIECES)),
            dma((3, EXPERTS)), dma((3, EXPERTS)), dma((3, SLOTS)), dma((3, SLOTS)),
            dma((2, SLOTS)), dma((2, SLOTS)), dma((2, EXPERTS)), dma((2, EXPERTS)),
        ],
        compiler_params=pltpu.CompilerParams(
            collective_id=0, has_side_effects=True, vmem_limit_bytes=52 * 1024 * 1024
        ),
        name="relay",
    )(*operands)


def per_device(
    act_in,
    saved_in,
    grad_in,
    norm_gain,
    w_gate,
    w_up,
    w_down,
    routes_fwd,
    gates_fwd,
    routes_bwd,
    gates_bwd,
):
    act_out, grad_out = run_relay(
        act_in[0],
        saved_in[0],
        grad_in[0],
        norm_gain,
        w_gate[0].T,
        w_up[0].T,
        w_down[0],
        routes_fwd.reshape(1, TOK),
        gates_fwd.reshape(1, TOK),
        routes_bwd.reshape(1, TOK),
        gates_bwd.reshape(1, TOK),
    )
    return (act_out[None], grad_out[None])


def solution(mesh):
    in_specs = (
        P("section", "expert", None),
        P("section", "expert", None),
        P("section", "expert", None),
        P("section", None),
        P("section", None, "expert"),
        P("section", None, "expert"),
        P("section", "expert", None),
        P("section", "expert", None),
        P("section", "expert", None),
        P("section", "expert", None),
        P("section", "expert", None),
    )
    out_specs = (P("section", "expert", None), P("section", "expert", None))
    return jax.shard_map(
        per_device, mesh=mesh, in_specs=in_specs, out_specs=out_specs, check_vma=False
    )
```

```python
import jax
import jax.numpy as jnp
from jax import lax
from jax.experimental import pallas as pl
from jax.experimental.pallas import tpu as pltpu
from jax.sharding import PartitionSpec as P

MESH = pl.DeviceIdType.MESH

SPLIT = 4
EXPERTS = 8
D = 2048
TOK = 128
UNITS = 192
PIECES = 3
PIECE = UNITS // PIECES
WIDE = UNITS * SPLIT
MAIN = 16
TAIL = 2
PACKED = EXPERTS * (MAIN + TAIL)
SLOTS = 16
FIRST_TAIL = SLOTS * MAIN
ROWS = SLOTS * (MAIN + TAIL)
RING = 16
BLOCKS = RING // SPLIT
TILE = 256

norm_eps = 1e-06

NT = (((1,), (1,)), ((), ()))


def way(block, place, there):
    apart = lax.rem(there - block + BLOCKS, BLOCKS)
    first = place == 0
    to_edge = jnp.logical_or(
        apart == 1,
        jnp.logical_or(
            jnp.logical_and(apart == 2, place >= 1), jnp.logical_and(apart == 0, first)
        ),
    )
    kind = jnp.where(
        apart == 0,
        jnp.where(first, 7, 4 + place),
        jnp.where(apart == 2, jnp.where(first, 4, 3 + place), place),
    )
    return jnp.where(to_edge, 0, 1), kind


def origin(block, place, slot):
    edge = place == 0
    kind = lax.rem(slot, 8)
    opposite = jnp.where(edge, 6, 4)
    apart = jnp.where(kind < 4, jnp.where(edge, 3, 1), jnp.where(kind <= opposite, 2, 0))
    source_place = jnp.where(
        kind < 4,
        kind,
        jnp.where(edge, jnp.where(kind == 7, 0, kind - 3), kind - 4),
    )
    return slot // 8, lax.rem(block + apart, BLOCKS), source_place


def relay_kernel(
    act_in, saved_in, grad_in, gain, wg_in, wu_in, wd_in, routes_f, gates_f, routes_b, gates_b,
    act_out, grad_out,
    x_new, dy, f_main, f_tail, b_main, b_tail, g_main, g_tail,
    home_f, home_ft, home_b, home_bt, scaled,
    xf, xft, xb, xbt, xg, xgt, wg, wu, wd, yf, yft, yb, ybt, hid_a, hid_b, tail_rows, own_tails,
    hop_send, hop_recv, w_local, w_send, w_recv,
    send_m, send_t, recv_m, recv_t, back_m, back_t, home_m, home_ts,
):
    me = lax.axis_index("expert")
    section = lax.axis_index("section")
    sections = lax.axis_size("section")
    after = lax.rem(section + 1, sections)
    ahead = lax.rem(section + sections - 1, sections)
    mirrored = lax.rem(section, 2) == 1
    x_lo = me // RING
    z = lax.rem(me, RING)
    turned = jnp.where(mirrored, RING - 1 - z, z)
    block = turned // SPLIT
    place = lax.rem(turned, SPLIT)
    edge = place == 0
    middle = place == 1
    computing = place < 2

    def device(x, its_block, its_place):
        along = its_block * SPLIT + its_place
        return x * RING + jnp.where(mirrored, RING - 1 - along, along)

    def neighbour(its_place):
        return device(x_lo, block, its_place)

    def expert_row(x, its_block):
        return x * BLOCKS + jnp.where(mirrored, BLOCKS - 1 - its_block, its_block)

    own_expert = expert_row(x_lo, block)

    def target_of(number):
        x = number // BLOCKS
        there = lax.rem(number, BLOCKS)
        member, kind = way(block, place, there)
        slot = x_lo * (SLOTS // 2) + kind
        return device(x, there, member), slot, expert_row(x, there)

    def source_of(slot):
        return device(*origin(block, place, slot))

    barrier = pltpu.get_barrier_semaphore()

    def signal(name, index):
        pl.semaphore_signal(barrier, inc=1, device_id={name: index}, device_id_type=MESH)

    signal("section", after)
    signal("section", ahead)

    def greet(number, carry):
        dest, _, _ = target_of(number)

        @pl.when(dest != me)
        def _():
            signal("expert", dest)

        return carry

    lax.fori_loop(0, EXPERTS, greet, 0)

    @pl.when(computing)
    def _():
        def greet_source(slot, carry):
            source = source_of(slot)

            @pl.when(source != me)
            def _():
                signal("expert", source)

            return carry

        lax.fori_loop(0, SLOTS, greet_source, 0)
        signal("expert", neighbour(1 - place))

    pl.semaphore_wait(barrier, jnp.where(computing, 7 + 15 + 1 + 2, 8 + 2))

    weights = ((wg_in, wg), (wu_in, wu), (wd_in, wd))

    def share_rows(share):
        return pl.ds(pl.multiple_of(share * UNITS, UNITS), UNITS)

    def piece_rows(start):
        return pl.ds(pl.multiple_of(start, PIECE), PIECE)

    def weight_copy(kind, piece, share, sent, dest, passed=False):
        there = weights[kind][1].at[piece_rows(share * UNITS + piece * PIECE)]
        return pltpu.make_async_remote_copy(
            src_ref=there if passed else weights[kind][0].at[piece_rows(piece * PIECE)],
            dst_ref=there,
            send_sem=w_send.at[sent, kind, piece],
            recv_sem=w_recv.at[share, kind, piece],
            device_id={"expert": dest},
            device_id_type=MESH,
        )

    def each_piece(body):
        for kind in range(3):

            def step(piece, carry):
                body(kind, piece)
                return carry

            lax.fori_loop(0, PIECES, step, 0)

    def hop(source, target, number, there):
        return pltpu.make_async_remote_copy(
            src_ref=source,
            dst_ref=target,
            send_sem=hop_send.at[number],
            recv_sem=hop_recv.at[number],
            device_id={"section": there},
            device_id_type=MESH,
        )

    each_piece(
        lambda kind, piece: weight_copy(
            kind, piece, place, 0, neighbour(jnp.where(middle, 0, 1))
        ).start()
    )

    for kind in range(3):
        own = weights[kind][0]

        @pl.when(computing)
        def _():
            pltpu.make_async_copy(
                own, weights[kind][1].at[share_rows(place)], w_local.at[kind]
            ).start()

    hop_act = hop(act_in, x_new, 0, after)
    hop_grad = hop(grad_in, dy, 1, ahead)
    hop_act.start()
    hop_grad.start()

    def one_hots(routes):
        down = lax.broadcasted_iota(jnp.int32, (TOK, TOK), 0)
        across = lax.broadcasted_iota(jnp.int32, (TOK, TOK), 1)
        row = routes[...].astype(jnp.float32)
        rows = jnp.broadcast_to(row, (TOK, TOK))
        column = jnp.sum(jnp.where(down == across, rows, 0.0), axis=1, keepdims=True)
        same = rows == column
        slot_row = jnp.sum(jnp.where(jnp.logical_and(same, down < across), 1.0, 0.0), axis=0, keepdims=True)
        slot_column = jnp.sum(jnp.where(jnp.logical_and(same, across < down), 1.0, 0.0), axis=1, keepdims=True)

        def packed_row(expert, slot):
            return jnp.where(
                slot < MAIN, expert * MAIN + slot, EXPERTS * MAIN + expert * TAIL + slot - MAIN
            ).astype(jnp.int32)

        pick_in = lax.broadcasted_iota(jnp.int32, (PACKED, TOK), 0) == packed_row(row, slot_row)
        pick_out = lax.broadcasted_iota(jnp.int32, (TOK, PACKED), 1) == packed_row(column, slot_column)
        return (
            jnp.where(pick_in, 1.0, 0.0).astype(jnp.bfloat16),
            jnp.where(pick_out, 1.0, 0.0).astype(jnp.bfloat16),
        )

    def as_column(row_ref):
        down = lax.broadcasted_iota(jnp.int32, (TOK, TOK), 0)
        across = lax.broadcasted_iota(jnp.int32, (TOK, TOK), 1)
        rows = jnp.broadcast_to(row_ref[...], (TOK, TOK))
        return jnp.sum(jnp.where(down == across, rows, 0.0), axis=1, keepdims=True)

    def inverse_scale(rows):
        values = rows[...].astype(jnp.float32)
        return lax.rsqrt(jnp.mean(values * values, axis=-1, keepdims=True) + norm_eps)

    def static_cols(step):
        return slice(step * TILE, (step + 1) * TILE)

    def pack(chooser, rows, inv_scale, main, tail):
        for step in range(D // TILE):
            part = rows[:, static_cols(step)]
            if inv_scale is not None:
                part = (part.astype(jnp.float32) * inv_scale * gain[:, static_cols(step)]).astype(
                    jnp.bfloat16
                )
            value = jnp.dot(chooser, part, preferred_element_type=jnp.float32)
            main[:, static_cols(step)] = value[: EXPERTS * MAIN].astype(jnp.bfloat16)
            own_tails[:, static_cols(step)] = value[EXPERTS * MAIN :]
        for expert in range(EXPERTS):
            tail[expert] = own_tails[expert * TAIL : (expert + 1) * TAIL, :].astype(jnp.bfloat16)

    streams = (
        (f_main, f_tail, xf, xft),
        (b_main, b_tail, xb, xbt),
        (g_main, g_tail, xg, xgt),
    )

    def main_rows(index):
        return pl.ds(pl.multiple_of(index * MAIN, MAIN), MAIN)

    def send_stream(stream):
        main_in, tail_in, main_there, tail_there = streams[stream]

        def body(number, carry):
            dest, slot, expert = target_of(number)
            pieces = (
                (main_in.at[main_rows(expert)], main_there.at[main_rows(slot)], send_m, recv_m),
                (tail_in.at[expert], tail_there.at[slot], send_t, recv_t),
            )
            for source, target, sent, got in pieces:

                @pl.when(dest == me)
                def _():
                    pltpu.make_async_copy(source, target, got.at[stream, slot]).start()

                @pl.when(dest != me)
                def _():
                    pltpu.make_async_remote_copy(
                        src_ref=source,
                        dst_ref=target,
                        send_sem=sent.at[stream, number],
                        recv_sem=got.at[stream, slot],
                        device_id={"expert": dest},
                        device_id_type=MESH,
                    ).start()

            return carry

        lax.fori_loop(0, EXPERTS, body, 0)

    chooser_b, chosen_b = one_hots(routes_b)
    inv_b = inverse_scale(saved_in)
    pack(chooser_b, saved_in, inv_b, b_main, b_tail)
    send_stream(1)

    hop_grad.wait_recv()
    pack(chooser_b, dy, None, g_main, g_tail)
    @pl.when(jnp.logical_not(middle))
    def _():
        send_stream(2)

    chooser_f, chosen_f = one_hots(routes_f)
    hop_act.wait_recv()
    pack(chooser_f, x_new, inverse_scale(x_new), f_main, f_tail)
    def wait_stream(stream):
        main_in, tail_in, main_there, tail_there = streams[stream]

        def body(slot, carry):
            pltpu.make_async_copy(
                main_in.at[main_rows(0)], main_there.at[main_rows(slot)], recv_m.at[stream, slot]
            ).wait()
            pltpu.make_async_copy(
                tail_in.at[0], tail_there.at[slot], recv_t.at[stream, slot]
            ).wait()
            return carry

        lax.fori_loop(0, SLOTS, body, 0)
        for slot in range(SLOTS):
            tail_rows[slot * TAIL : (slot + 1) * TAIL, :] = tail_there[slot].astype(jnp.float32)
        main_there[FIRST_TAIL:ROWS, :] = tail_rows[...].astype(jnp.bfloat16)

    def send_back(which, main_here, tail_here, main_home, tail_home):
        def body(slot, carry):
            source = source_of(slot)
            pieces = (
                (main_here.at[main_rows(slot)], main_home.at[main_rows(own_expert)], back_m, home_m),
                (tail_here.at[slot], tail_home.at[own_expert], back_t, home_ts),
            )
            for here, target, sent, got in pieces:

                @pl.when(source == me)
                def _():
                    pltpu.make_async_copy(here, target, got.at[which, own_expert]).start()

                @pl.when(source != me)
                def _():
                    pltpu.make_async_remote_copy(
                        src_ref=here,
                        dst_ref=target,
                        send_sem=sent.at[which, slot],
                        recv_sem=got.at[which, own_expert],
                        device_id={"expert": source},
                        device_id_type=MESH,
                    ).start()

            return carry

        lax.fori_loop(0, SLOTS, body, 0)

    def cols(step):
        return pl.ds(pl.multiple_of(step * TILE, TILE), TILE)

    def put_result(main_here, step, value):
        main_here[:, cols(step)] = value[:FIRST_TAIL].astype(jnp.bfloat16)
        tail_rows[:, cols(step)] = value[FIRST_TAIL:]

    def put_tails(tail_here):
        for slot in range(SLOTS):
            tail_here[slot] = tail_rows[slot * TAIL : (slot + 1) * TAIL, :].astype(jnp.bfloat16)

    def dot_nt(left, right):
        return lax.dot_general(left, right, NT, preferred_element_type=jnp.float32)

    def dot_nn(left, right):
        return jnp.dot(left, right, preferred_element_type=jnp.float32)

    @pl.when(middle)
    def _():
        def pass_on(kind, piece):
            for share in (2, 3):
                weight_copy(kind, piece, share, 0, neighbour(0)).wait_recv()
                weight_copy(kind, piece, share, share - 1, neighbour(0), True).start()

        each_piece(pass_on)
        send_stream(2)

    @pl.when(computing)
    def _():
        for kind in range(3):
            own = weights[kind][0]
            held = weights[kind][1].at[share_rows(place)]
            pltpu.make_async_copy(own, held, w_local.at[kind]).wait()

        each_piece(
            lambda kind, piece: weight_copy(kind, piece, 1 - place, 0, neighbour(0)).wait_recv()
        )

        @pl.when(edge)
        def _():
            def arrived(kind, piece):
                for share in (2, 3):
                    weight_copy(kind, piece, share, 0, neighbour(0)).wait_recv()

            each_piece(arrived)

    @pl.when(jnp.logical_not(computing))
    def _():
        each_piece(lambda kind, piece: weight_copy(kind, piece, 0, 0, neighbour(0)).wait_send())

    send_stream(0)

    @pl.when(computing)
    def _():
        wait_stream(1)
        wait_stream(2)

        def backward_hidden(step, carry):
            gate_pre = dot_nt(xb[...], wg[cols(step), :])
            up_pre = dot_nt(xb[...], wu[cols(step), :])
            d_hidden = dot_nt(xg[...], wd[cols(step), :])
            sigma = jax.nn.sigmoid(gate_pre)
            hid_a[:, cols(step)] = (
                d_hidden * up_pre * (sigma * (1.0 + gate_pre * (1.0 - sigma)))
            ).astype(jnp.bfloat16)
            hid_b[:, cols(step)] = (d_hidden * (gate_pre * sigma)).astype(jnp.bfloat16)
            return carry

        lax.fori_loop(0, WIDE // TILE, backward_hidden, 0)

        def backward_out(step, carry):
            value = dot_nn(hid_a[...], wg[:, cols(step)]) + dot_nn(hid_b[...], wu[:, cols(step)])
            put_result(yb, step, value)
            return carry

        lax.fori_loop(0, D // TILE, backward_out, 0)
        put_tails(ybt)
        send_back(1, yb, ybt, home_b, home_bt)

        wait_stream(0)

        def forward_hidden(step, carry):
            gate_pre = dot_nt(xf[...], wg[cols(step), :])
            up_pre = dot_nt(xf[...], wu[cols(step), :])
            hid_a[:, cols(step)] = (gate_pre * jax.nn.sigmoid(gate_pre) * up_pre).astype(
                jnp.bfloat16
            )
            return carry

        lax.fori_loop(0, WIDE // TILE, forward_hidden, 0)

        def forward_out(step, carry):
            put_result(yf, step, dot_nn(hid_a[...], wd[:, cols(step)]))
            return carry

        lax.fori_loop(0, D // TILE, forward_out, 0)
        put_tails(yft)
        send_back(0, yf, yft, home_f, home_ft)

    homes = ((yf, yft, home_f, home_ft), (yb, ybt, home_b, home_bt))

    def wait_home(which):
        main_here, tail_here, main_home, tail_home = homes[which]

        def body(expert, carry):
            pltpu.make_async_copy(
                main_here.at[main_rows(0)], main_home.at[main_rows(expert)], home_m.at[which, expert]
            ).wait()
            pltpu.make_async_copy(
                tail_here.at[0], tail_home.at[expert], home_ts.at[which, expert]
            ).wait()
            return carry

        lax.fori_loop(0, EXPERTS, body, 0)
        for expert in range(EXPERTS):
            own_tails[expert * TAIL : (expert + 1) * TAIL, :] = tail_home[expert].astype(jnp.float32)
        main_home[EXPERTS * MAIN :, :] = own_tails[...].astype(jnp.bfloat16)

    gate_f = as_column(gates_f)
    gate_b = as_column(gates_b)
    wait_home(1)
    total = jnp.zeros((TOK, 1), jnp.float32)
    for step in range(D // TILE):
        part = static_cols(step)
        value = dot_nn(chosen_b, home_b[:, part]) * gate_b * gain[:, part]
        scaled[:, part] = value
        total = total + jnp.sum(
            value * saved_in[:, part].astype(jnp.float32), axis=-1, keepdims=True
        )
    inv_scale = inverse_scale(saved_in)
    fold = inv_scale * inv_scale * (total / D)
    for step in range(D // TILE):
        part = static_cols(step)
        d_input = inv_scale * (scaled[:, part] - saved_in[:, part].astype(jnp.float32) * fold)
        grad_out[:, part] = (dy[:, part].astype(jnp.float32) + d_input).astype(jnp.bfloat16)

    wait_home(0)
    for step in range(D // TILE):
        part = static_cols(step)
        mixed = dot_nn(chosen_f, home_f[:, part]) * gate_f
        act_out[:, part] = (x_new[:, part].astype(jnp.float32) + mixed).astype(jnp.bfloat16)

    hop_act.wait_send()
    hop_grad.wait_send()

    for stream in range(3):
        main_in, tail_in, main_there, tail_there = streams[stream]

        def left(number, carry):
            dest, _, expert = target_of(number)

            @pl.when(dest != me)
            def _():
                pltpu.make_async_copy(
                    main_in.at[main_rows(expert)], main_there.at[main_rows(0)],
                    send_m.at[stream, number],
                ).wait()
                pltpu.make_async_copy(
                    tail_in.at[expert], tail_there.at[0], send_t.at[stream, number]
                ).wait()

            return carry

        lax.fori_loop(0, EXPERTS, left, 0)

    @pl.when(computing)
    def _():
        each_piece(lambda kind, piece: weight_copy(kind, piece, 0, 0, neighbour(0)).wait_send())

    @pl.when(middle)
    def _():
        def passed_on(kind, piece):
            for sent in (1, 2):
                weight_copy(kind, piece, 0, sent, neighbour(0)).wait_send()

        each_piece(passed_on)

    @pl.when(computing)
    def _():
        for which in range(2):
            main_here, tail_here, main_home, tail_home = homes[which]

            def gone(slot, carry):
                source = source_of(slot)

                @pl.when(source != me)
                def _():
                    pltpu.make_async_copy(
                        main_here.at[main_rows(slot)], main_home.at[main_rows(0)],
                        back_m.at[which, slot],
                    ).wait()
                    pltpu.make_async_copy(
                        tail_here.at[slot], tail_home.at[0], back_t.at[which, slot]
                    ).wait()

                return carry

            lax.fori_loop(0, SLOTS, gone, 0)


def run_relay(*operands):
    bf16 = jnp.bfloat16
    vmem = pl.BlockSpec(memory_space=pltpu.VMEM)
    anywhere = pl.BlockSpec(memory_space=pltpu.HBM)
    dma = pltpu.SemaphoreType.DMA
    tokens = pltpu.VMEM((TOK, D), bf16)
    packed_main = pltpu.VMEM((EXPERTS * MAIN, D), bf16)
    packed_tail = pltpu.VMEM((EXPERTS, TAIL, D), bf16)
    home_main = pltpu.VMEM((PACKED, D), bf16)
    rows_in = pltpu.VMEM((ROWS, D), bf16)
    tails_in = pltpu.VMEM((SLOTS, TAIL, D), bf16)
    weight = pltpu.VMEM((WIDE, D), bf16)
    main_out = pltpu.VMEM((FIRST_TAIL, D), bf16)
    hidden = pltpu.VMEM((ROWS, WIDE), bf16)
    out = jax.ShapeDtypeStruct((TOK, D), bf16)
    return pl.pallas_call(
        relay_kernel,
        out_shape=(out, out),
        in_specs=[anywhere, vmem, anywhere, vmem, anywhere, anywhere, anywhere, vmem, vmem, vmem, vmem],
        out_specs=(vmem, vmem),
        scratch_shapes=[
            tokens, tokens, packed_main, packed_tail, packed_main, packed_tail, packed_main, packed_tail,
            home_main, packed_tail, home_main, packed_tail, pltpu.VMEM((TOK, D), jnp.float32),
            rows_in, tails_in, rows_in, tails_in, rows_in, tails_in,
            weight, weight, weight,
            main_out, tails_in, main_out, tails_in,
            hidden, hidden,
            pltpu.VMEM((ROWS - FIRST_TAIL, D), jnp.float32),
            pltpu.VMEM((EXPERTS * TAIL, D), jnp.float32),
            dma((2,)), dma((2,)), dma((3,)), dma((3, 3, PIECES)), dma((SPLIT, 3, PIECES)),
            dma((3, EXPERTS)), dma((3, EXPERTS)), dma((3, SLOTS)), dma((3, SLOTS)),
            dma((2, SLOTS)), dma((2, SLOTS)), dma((2, EXPERTS)), dma((2, EXPERTS)),
        ],
        compiler_params=pltpu.CompilerParams(
            collective_id=0, has_side_effects=True, vmem_limit_bytes=52 * 1024 * 1024
        ),
        name="relay",
    )(*operands)


def per_device(
    act_in,
    saved_in,
    grad_in,
    norm_gain,
    w_gate,
    w_up,
    w_down,
    routes_fwd,
    gates_fwd,
    routes_bwd,
    gates_bwd,
):
    act_out, grad_out = run_relay(
        act_in[0],
        saved_in[0],
        grad_in[0],
        norm_gain,
        w_gate[0].T,
        w_up[0].T,
        w_down[0],
        routes_fwd.reshape(1, TOK),
        gates_fwd.reshape(1, TOK),
        routes_bwd.reshape(1, TOK),
        gates_bwd.reshape(1, TOK),
    )
    return (act_out[None], grad_out[None])


def solution(mesh):
    in_specs = (
        P("section", "expert", None),
        P("section", "expert", None),
        P("section", "expert", None),
        P("section", None),
        P("section", None, "expert"),
        P("section", None, "expert"),
        P("section", "expert", None),
        P("section", "expert", None),
        P("section", "expert", None),
        P("section", "expert", None),
        P("section", "expert", None),
    )
    out_specs = (P("section", "expert", None), P("section", "expert", None))
    return jax.shard_map(
        per_device, mesh=mesh, in_specs=in_specs, out_specs=out_specs, check_vma=False
    )
```

```python
import jax
import jax.numpy as jnp
from jax import lax
from jax.experimental import pallas as pl
from jax.experimental.pallas import tpu as pltpu
from jax.sharding import PartitionSpec as P

MESH = pl.DeviceIdType.MESH

SPLIT = 4
EXPERTS = 8
D = 2048
TOK = 128
UNITS = 192
PIECES = 2
PIECE = UNITS // PIECES
WIDE = UNITS * SPLIT
MAIN = 16
TAIL = 2
PACKED = EXPERTS * (MAIN + TAIL)
SLOTS = 16
FIRST_TAIL = SLOTS * MAIN
ROWS = SLOTS * (MAIN + TAIL)
RING = 16
BLOCKS = RING // SPLIT
TILE = 256

norm_eps = 1e-06

NT = (((1,), (1,)), ((), ()))


def way(block, place, there):
    apart = lax.rem(there - block + BLOCKS, BLOCKS)
    first = place == 0
    to_edge = jnp.logical_or(
        apart == 1,
        jnp.logical_or(
            jnp.logical_and(apart == 2, place >= 1), jnp.logical_and(apart == 0, first)
        ),
    )
    kind = jnp.where(
        apart == 0,
        jnp.where(first, 7, 4 + place),
        jnp.where(apart == 2, jnp.where(first, 4, 3 + place), place),
    )
    return jnp.where(to_edge, 0, 1), kind


def origin(block, place, slot):
    edge = place == 0
    kind = lax.rem(slot, 8)
    opposite = jnp.where(edge, 6, 4)
    apart = jnp.where(kind < 4, jnp.where(edge, 3, 1), jnp.where(kind <= opposite, 2, 0))
    source_place = jnp.where(
        kind < 4,
        kind,
        jnp.where(edge, jnp.where(kind == 7, 0, kind - 3), kind - 4),
    )
    return slot // 8, lax.rem(block + apart, BLOCKS), source_place


def relay_kernel(
    act_in, saved_in, grad_in, gain, wg_in, wu_in, wd_in, routes_f, gates_f, routes_b, gates_b,
    act_out, grad_out,
    x_new, dy, f_main, f_tail, b_main, b_tail, g_main, g_tail,
    home_f, home_ft, home_b, home_bt, scaled,
    xf, xft, xb, xbt, xg, xgt, wg, wu, wd, yf, yft, yb, ybt, hid_a, hid_b, tail_rows, own_tails,
    hop_send, hop_recv, w_local, w_send, w_recv,
    send_m, send_t, recv_m, recv_t, back_m, back_t, home_m, home_ts,
):
    me = lax.axis_index("expert")
    section = lax.axis_index("section")
    sections = lax.axis_size("section")
    after = lax.rem(section + 1, sections)
    ahead = lax.rem(section + sections - 1, sections)
    mirrored = lax.rem(section, 2) == 1
    x_lo = me // RING
    z = lax.rem(me, RING)
    turned = jnp.where(mirrored, RING - 1 - z, z)
    block = turned // SPLIT
    place = lax.rem(turned, SPLIT)
    edge = place == 0
    middle = place == 1
    computing = place < 2

    def device(x, its_block, its_place):
        along = its_block * SPLIT + its_place
        return x * RING + jnp.where(mirrored, RING - 1 - along, along)

    def neighbour(its_place):
        return device(x_lo, block, its_place)

    def expert_row(x, its_block):
        return x * BLOCKS + jnp.where(mirrored, BLOCKS - 1 - its_block, its_block)

    own_expert = expert_row(x_lo, block)

    def target_of(number):
        x = number // BLOCKS
        there = lax.rem(number, BLOCKS)
        member, kind = way(block, place, there)
        slot = x_lo * (SLOTS // 2) + kind
        return device(x, there, member), slot, expert_row(x, there)

    def source_of(slot):
        return device(*origin(block, place, slot))

    barrier = pltpu.get_barrier_semaphore()

    def signal(name, index):
        pl.semaphore_signal(barrier, inc=1, device_id={name: index}, device_id_type=MESH)

    signal("section", after)
    signal("section", ahead)

    def greet(number, carry):
        dest, _, _ = target_of(number)

        @pl.when(dest != me)
        def _():
            signal("expert", dest)

        return carry

    lax.fori_loop(0, EXPERTS, greet, 0)

    @pl.when(computing)
    def _():
        def greet_source(slot, carry):
            source = source_of(slot)

            @pl.when(source != me)
            def _():
                signal("expert", source)

            return carry

        lax.fori_loop(0, SLOTS, greet_source, 0)
        signal("expert", neighbour(1 - place))

    pl.semaphore_wait(barrier, jnp.where(computing, 7 + 15 + 1 + 2, 8 + 2))

    weights = ((wg_in, wg), (wu_in, wu), (wd_in, wd))

    def share_rows(share):
        return pl.ds(pl.multiple_of(share * UNITS, UNITS), UNITS)

    def piece_rows(start):
        return pl.ds(pl.multiple_of(start, PIECE), PIECE)

    def weight_copy(kind, piece, share, sent, dest, passed=False):
        there = weights[kind][1].at[piece_rows(share * UNITS + piece * PIECE)]
        return pltpu.make_async_remote_copy(
            src_ref=there if passed else weights[kind][0].at[piece_rows(piece * PIECE)],
            dst_ref=there,
            send_sem=w_send.at[sent, kind, piece],
            recv_sem=w_recv.at[share, kind, piece],
            device_id={"expert": dest},
            device_id_type=MESH,
        )

    def each_piece(body):
        for kind in range(3):

            def step(piece, carry):
                body(kind, piece)
                return carry

            lax.fori_loop(0, PIECES, step, 0)

    def hop(source, target, number, there):
        return pltpu.make_async_remote_copy(
            src_ref=source,
            dst_ref=target,
            send_sem=hop_send.at[number],
            recv_sem=hop_recv.at[number],
            device_id={"section": there},
            device_id_type=MESH,
        )

    each_piece(
        lambda kind, piece: weight_copy(
            kind, piece, place, 0, neighbour(jnp.where(middle, 0, 1))
        ).start()
    )

    for kind in range(3):
        own = weights[kind][0]

        @pl.when(computing)
        def _():
            pltpu.make_async_copy(
                own, weights[kind][1].at[share_rows(place)], w_local.at[kind]
            ).start()

    hop_act = hop(act_in, x_new, 0, after)
    hop_grad = hop(grad_in, dy, 1, ahead)
    hop_act.start()
    hop_grad.start()

    def one_hots(routes):
        down = lax.broadcasted_iota(jnp.int32, (TOK, TOK), 0)
        across = lax.broadcasted_iota(jnp.int32, (TOK, TOK), 1)
        row = routes[...].astype(jnp.float32)
        rows = jnp.broadcast_to(row, (TOK, TOK))
        column = jnp.sum(jnp.where(down == across, rows, 0.0), axis=1, keepdims=True)
        same = rows == column
        slot_row = jnp.sum(jnp.where(jnp.logical_and(same, down < across), 1.0, 0.0), axis=0, keepdims=True)
        slot_column = jnp.sum(jnp.where(jnp.logical_and(same, across < down), 1.0, 0.0), axis=1, keepdims=True)

        def packed_row(expert, slot):
            return jnp.where(
                slot < MAIN, expert * MAIN + slot, EXPERTS * MAIN + expert * TAIL + slot - MAIN
            ).astype(jnp.int32)

        pick_in = lax.broadcasted_iota(jnp.int32, (PACKED, TOK), 0) == packed_row(row, slot_row)
        pick_out = lax.broadcasted_iota(jnp.int32, (TOK, PACKED), 1) == packed_row(column, slot_column)
        return (
            jnp.where(pick_in, 1.0, 0.0).astype(jnp.bfloat16),
            jnp.where(pick_out, 1.0, 0.0).astype(jnp.bfloat16),
        )

    def as_column(row_ref):
        down = lax.broadcasted_iota(jnp.int32, (TOK, TOK), 0)
        across = lax.broadcasted_iota(jnp.int32, (TOK, TOK), 1)
        rows = jnp.broadcast_to(row_ref[...], (TOK, TOK))
        return jnp.sum(jnp.where(down == across, rows, 0.0), axis=1, keepdims=True)

    def inverse_scale(rows):
        values = rows[...].astype(jnp.float32)
        return lax.rsqrt(jnp.mean(values * values, axis=-1, keepdims=True) + norm_eps)

    def static_cols(step):
        return slice(step * TILE, (step + 1) * TILE)

    def pack(chooser, rows, inv_scale, main, tail):
        for step in range(D // TILE):
            part = rows[:, static_cols(step)]
            if inv_scale is not None:
                part = (part.astype(jnp.float32) * inv_scale * gain[:, static_cols(step)]).astype(
                    jnp.bfloat16
                )
            value = jnp.dot(chooser, part, preferred_element_type=jnp.float32)
            main[:, static_cols(step)] = value[: EXPERTS * MAIN].astype(jnp.bfloat16)
            own_tails[:, static_cols(step)] = value[EXPERTS * MAIN :]
        for expert in range(EXPERTS):
            tail[expert] = own_tails[expert * TAIL : (expert + 1) * TAIL, :].astype(jnp.bfloat16)

    streams = (
        (f_main, f_tail, xf, xft),
        (b_main, b_tail, xb, xbt),
        (g_main, g_tail, xg, xgt),
    )

    def main_rows(index):
        return pl.ds(pl.multiple_of(index * MAIN, MAIN), MAIN)

    def send_stream(stream):
        main_in, tail_in, main_there, tail_there = streams[stream]

        def body(number, carry):
            dest, slot, expert = target_of(number)
            pieces = (
                (main_in.at[main_rows(expert)], main_there.at[main_rows(slot)], send_m, recv_m),
                (tail_in.at[expert], tail_there.at[slot], send_t, recv_t),
            )
            for source, target, sent, got in pieces:

                @pl.when(dest == me)
                def _():
                    pltpu.make_async_copy(source, target, got.at[stream, slot]).start()

                @pl.when(dest != me)
                def _():
                    pltpu.make_async_remote_copy(
                        src_ref=source,
                        dst_ref=target,
                        send_sem=sent.at[stream, number],
                        recv_sem=got.at[stream, slot],
                        device_id={"expert": dest},
                        device_id_type=MESH,
                    ).start()

            return carry

        lax.fori_loop(0, EXPERTS, body, 0)

    chooser_b, chosen_b = one_hots(routes_b)
    inv_b = inverse_scale(saved_in)
    pack(chooser_b, saved_in, inv_b, b_main, b_tail)
    send_stream(1)

    hop_grad.wait_recv()
    pack(chooser_b, dy, None, g_main, g_tail)
    @pl.when(jnp.logical_not(middle))
    def _():
        send_stream(2)

    chooser_f, chosen_f = one_hots(routes_f)
    hop_act.wait_recv()
    pack(chooser_f, x_new, inverse_scale(x_new), f_main, f_tail)
    def wait_stream(stream):
        main_in, tail_in, main_there, tail_there = streams[stream]

        def body(slot, carry):
            pltpu.make_async_copy(
                main_in.at[main_rows(0)], main_there.at[main_rows(slot)], recv_m.at[stream, slot]
            ).wait()
            pltpu.make_async_copy(
                tail_in.at[0], tail_there.at[slot], recv_t.at[stream, slot]
            ).wait()
            return carry

        lax.fori_loop(0, SLOTS, body, 0)
        for slot in range(SLOTS):
            tail_rows[slot * TAIL : (slot + 1) * TAIL, :] = tail_there[slot].astype(jnp.float32)
        main_there[FIRST_TAIL:ROWS, :] = tail_rows[...].astype(jnp.bfloat16)

    def send_back(which, main_here, tail_here, main_home, tail_home):
        def body(slot, carry):
            source = source_of(slot)
            pieces = (
                (main_here.at[main_rows(slot)], main_home.at[main_rows(own_expert)], back_m, home_m),
                (tail_here.at[slot], tail_home.at[own_expert], back_t, home_ts),
            )
            for here, target, sent, got in pieces:

                @pl.when(source == me)
                def _():
                    pltpu.make_async_copy(here, target, got.at[which, own_expert]).start()

                @pl.when(source != me)
                def _():
                    pltpu.make_async_remote_copy(
                        src_ref=here,
                        dst_ref=target,
                        send_sem=sent.at[which, slot],
                        recv_sem=got.at[which, own_expert],
                        device_id={"expert": source},
                        device_id_type=MESH,
                    ).start()

            return carry

        lax.fori_loop(0, SLOTS, body, 0)

    def cols(step):
        return pl.ds(pl.multiple_of(step * TILE, TILE), TILE)

    def put_result(main_here, step, value):
        main_here[:, cols(step)] = value[:FIRST_TAIL].astype(jnp.bfloat16)
        tail_rows[:, cols(step)] = value[FIRST_TAIL:]

    def put_tails(tail_here):
        for slot in range(SLOTS):
            tail_here[slot] = tail_rows[slot * TAIL : (slot + 1) * TAIL, :].astype(jnp.bfloat16)

    def dot_nt(left, right):
        return lax.dot_general(left, right, NT, preferred_element_type=jnp.float32)

    def dot_nn(left, right):
        return jnp.dot(left, right, preferred_element_type=jnp.float32)

    @pl.when(middle)
    def _():
        def pass_on(kind, piece):
            for share in (2, 3):
                weight_copy(kind, piece, share, 0, neighbour(0)).wait_recv()
                weight_copy(kind, piece, share, share - 1, neighbour(0), True).start()

        each_piece(pass_on)
        send_stream(2)

    @pl.when(computing)
    def _():
        for kind in range(3):
            own = weights[kind][0]
            held = weights[kind][1].at[share_rows(place)]
            pltpu.make_async_copy(own, held, w_local.at[kind]).wait()

        each_piece(
            lambda kind, piece: weight_copy(kind, piece, 1 - place, 0, neighbour(0)).wait_recv()
        )

        @pl.when(edge)
        def _():
            def arrived(kind, piece):
                for share in (2, 3):
                    weight_copy(kind, piece, share, 0, neighbour(0)).wait_recv()

            each_piece(arrived)

    @pl.when(jnp.logical_not(computing))
    def _():
        each_piece(lambda kind, piece: weight_copy(kind, piece, 0, 0, neighbour(0)).wait_send())

    send_stream(0)

    @pl.when(computing)
    def _():
        wait_stream(1)
        wait_stream(2)

        def backward_hidden(step, carry):
            gate_pre = dot_nt(xb[...], wg[cols(step), :])
            up_pre = dot_nt(xb[...], wu[cols(step), :])
            d_hidden = dot_nt(xg[...], wd[cols(step), :])
            sigma = jax.nn.sigmoid(gate_pre)
            hid_a[:, cols(step)] = (
                d_hidden * up_pre * (sigma * (1.0 + gate_pre * (1.0 - sigma)))
            ).astype(jnp.bfloat16)
            hid_b[:, cols(step)] = (d_hidden * (gate_pre * sigma)).astype(jnp.bfloat16)
            return carry

        lax.fori_loop(0, WIDE // TILE, backward_hidden, 0)

        def backward_out(step, carry):
            value = dot_nn(hid_a[...], wg[:, cols(step)]) + dot_nn(hid_b[...], wu[:, cols(step)])
            put_result(yb, step, value)
            return carry

        lax.fori_loop(0, D // TILE, backward_out, 0)
        put_tails(ybt)
        send_back(1, yb, ybt, home_b, home_bt)

        wait_stream(0)

        def forward_hidden(step, carry):
            gate_pre = dot_nt(xf[...], wg[cols(step), :])
            up_pre = dot_nt(xf[...], wu[cols(step), :])
            hid_a[:, cols(step)] = (gate_pre * jax.nn.sigmoid(gate_pre) * up_pre).astype(
                jnp.bfloat16
            )
            return carry

        lax.fori_loop(0, WIDE // TILE, forward_hidden, 0)

        def forward_out(step, carry):
            put_result(yf, step, dot_nn(hid_a[...], wd[:, cols(step)]))
            return carry

        lax.fori_loop(0, D // TILE, forward_out, 0)
        put_tails(yft)
        send_back(0, yf, yft, home_f, home_ft)

    homes = ((yf, yft, home_f, home_ft), (yb, ybt, home_b, home_bt))

    def wait_home(which):
        main_here, tail_here, main_home, tail_home = homes[which]

        def body(expert, carry):
            pltpu.make_async_copy(
                main_here.at[main_rows(0)], main_home.at[main_rows(expert)], home_m.at[which, expert]
            ).wait()
            pltpu.make_async_copy(
                tail_here.at[0], tail_home.at[expert], home_ts.at[which, expert]
            ).wait()
            return carry

        lax.fori_loop(0, EXPERTS, body, 0)
        for expert in range(EXPERTS):
            own_tails[expert * TAIL : (expert + 1) * TAIL, :] = tail_home[expert].astype(jnp.float32)
        main_home[EXPERTS * MAIN :, :] = own_tails[...].astype(jnp.bfloat16)

    gate_f = as_column(gates_f)
    gate_b = as_column(gates_b)
    wait_home(1)
    total = jnp.zeros((TOK, 1), jnp.float32)
    for step in range(D // TILE):
        part = static_cols(step)
        value = dot_nn(chosen_b, home_b[:, part]) * gate_b * gain[:, part]
        scaled[:, part] = value
        total = total + jnp.sum(
            value * saved_in[:, part].astype(jnp.float32), axis=-1, keepdims=True
        )
    inv_scale = inverse_scale(saved_in)
    fold = inv_scale * inv_scale * (total / D)
    for step in range(D // TILE):
        part = static_cols(step)
        d_input = inv_scale * (scaled[:, part] - saved_in[:, part].astype(jnp.float32) * fold)
        grad_out[:, part] = (dy[:, part].astype(jnp.float32) + d_input).astype(jnp.bfloat16)

    wait_home(0)
    for step in range(D // TILE):
        part = static_cols(step)
        mixed = dot_nn(chosen_f, home_f[:, part]) * gate_f
        act_out[:, part] = (x_new[:, part].astype(jnp.float32) + mixed).astype(jnp.bfloat16)

    hop_act.wait_send()
    hop_grad.wait_send()

    for stream in range(3):
        main_in, tail_in, main_there, tail_there = streams[stream]

        def left(number, carry):
            dest, _, expert = target_of(number)

            @pl.when(dest != me)
            def _():
                pltpu.make_async_copy(
                    main_in.at[main_rows(expert)], main_there.at[main_rows(0)],
                    send_m.at[stream, number],
                ).wait()
                pltpu.make_async_copy(
                    tail_in.at[expert], tail_there.at[0], send_t.at[stream, number]
                ).wait()

            return carry

        lax.fori_loop(0, EXPERTS, left, 0)

    @pl.when(computing)
    def _():
        each_piece(lambda kind, piece: weight_copy(kind, piece, 0, 0, neighbour(0)).wait_send())

    @pl.when(middle)
    def _():
        def passed_on(kind, piece):
            for sent in (1, 2):
                weight_copy(kind, piece, 0, sent, neighbour(0)).wait_send()

        each_piece(passed_on)

    @pl.when(computing)
    def _():
        for which in range(2):
            main_here, tail_here, main_home, tail_home = homes[which]

            def gone(slot, carry):
                source = source_of(slot)

                @pl.when(source != me)
                def _():
                    pltpu.make_async_copy(
                        main_here.at[main_rows(slot)], main_home.at[main_rows(0)],
                        back_m.at[which, slot],
                    ).wait()
                    pltpu.make_async_copy(
                        tail_here.at[slot], tail_home.at[0], back_t.at[which, slot]
                    ).wait()

                return carry

            lax.fori_loop(0, SLOTS, gone, 0)


def run_relay(*operands):
    bf16 = jnp.bfloat16
    vmem = pl.BlockSpec(memory_space=pltpu.VMEM)
    anywhere = pl.BlockSpec(memory_space=pltpu.HBM)
    dma = pltpu.SemaphoreType.DMA
    tokens = pltpu.VMEM((TOK, D), bf16)
    packed_main = pltpu.VMEM((EXPERTS * MAIN, D), bf16)
    packed_tail = pltpu.VMEM((EXPERTS, TAIL, D), bf16)
    home_main = pltpu.VMEM((PACKED, D), bf16)
    rows_in = pltpu.VMEM((ROWS, D), bf16)
    tails_in = pltpu.VMEM((SLOTS, TAIL, D), bf16)
    weight = pltpu.VMEM((WIDE, D), bf16)
    main_out = pltpu.VMEM((FIRST_TAIL, D), bf16)
    hidden = pltpu.VMEM((ROWS, WIDE), bf16)
    out = jax.ShapeDtypeStruct((TOK, D), bf16)
    return pl.pallas_call(
        relay_kernel,
        out_shape=(out, out),
        in_specs=[anywhere, vmem, anywhere, vmem, anywhere, anywhere, anywhere, vmem, vmem, vmem, vmem],
        out_specs=(vmem, vmem),
        scratch_shapes=[
            tokens, tokens, packed_main, packed_tail, packed_main, packed_tail, packed_main, packed_tail,
            home_main, packed_tail, home_main, packed_tail, pltpu.VMEM((TOK, D), jnp.float32),
            rows_in, tails_in, rows_in, tails_in, rows_in, tails_in,
            weight, weight, weight,
            main_out, tails_in, main_out, tails_in,
            hidden, hidden,
            pltpu.VMEM((ROWS - FIRST_TAIL, D), jnp.float32),
            pltpu.VMEM((EXPERTS * TAIL, D), jnp.float32),
            dma((2,)), dma((2,)), dma((3,)), dma((3, 3, PIECES)), dma((SPLIT, 3, PIECES)),
            dma((3, EXPERTS)), dma((3, EXPERTS)), dma((3, SLOTS)), dma((3, SLOTS)),
            dma((2, SLOTS)), dma((2, SLOTS)), dma((2, EXPERTS)), dma((2, EXPERTS)),
        ],
        compiler_params=pltpu.CompilerParams(
            collective_id=0, has_side_effects=True, vmem_limit_bytes=52 * 1024 * 1024
        ),
        name="relay",
    )(*operands)


def per_device(
    act_in,
    saved_in,
    grad_in,
    norm_gain,
    w_gate,
    w_up,
    w_down,
    routes_fwd,
    gates_fwd,
    routes_bwd,
    gates_bwd,
):
    act_out, grad_out = run_relay(
        act_in[0],
        saved_in[0],
        grad_in[0],
        norm_gain,
        w_gate[0].T,
        w_up[0].T,
        w_down[0],
        routes_fwd.reshape(1, TOK),
        gates_fwd.reshape(1, TOK),
        routes_bwd.reshape(1, TOK),
        gates_bwd.reshape(1, TOK),
    )
    return (act_out[None], grad_out[None])


def solution(mesh):
    in_specs = (
        P("section", "expert", None),
        P("section", "expert", None),
        P("section", "expert", None),
        P("section", None),
        P("section", None, "expert"),
        P("section", None, "expert"),
        P("section", "expert", None),
        P("section", "expert", None),
        P("section", "expert", None),
        P("section", "expert", None),
        P("section", "expert", None),
    )
    out_specs = (P("section", "expert", None), P("section", "expert", None))
    return jax.shard_map(
        per_device, mesh=mesh, in_specs=in_specs, out_specs=out_specs, check_vma=False
    )
```
